32 devices in a mesh: grid: 4 (over y, core), tile: 8 (over z, x).
Axes of the slice: x: 2, y: 2, z: 4, core: 2. Of those that a mesh axis runs over, the one named last changes fastest.
Arguments:
- state_field: float32 [4, 128, 4, 4, 4, 4, 128], P('grid', 'tile'), may hold values from -6 to 6
- levels: int32 [4, 6], P('grid'), may hold values from 1 to 4
- sign_bits: int32 [4], P('grid'), may hold values from 0 to 1
Outputs:
- combined_field: float32 [4, 128, 4, 4, 4, 4, 128], P('grid', 'tile')
The draws below stay inside these ranges and needn't reach their ends.
All inputs are finite; a program needn't handle non-finite values.
Results may differ from the reference program's by a relative error of at most 0.0003.
Values sent between devices are 32-bit elements; how exact they have to be, the bound alone decides.
A program may use at most 64 MiB of HBM per device.

```python
import jax
import jax.numpy as jnp
import numpy as np
from jax import lax

Q = 4
L = 128
STEPS = 4
GRIDS = 4
NX = 128


def set_ends(values, key, low, top_value):
    longest = values.shape.index(max(values.shape))
    spots = []
    for shift in (0, 1):
        where = [jax.random.randint(jax.random.fold_in(key, axis), (), 0, length) for axis, length in enumerate(values.shape)]
        where[longest] = (where[longest] + shift) % values.shape[longest]
        spots.append(tuple(where))
    return values.at[spots[0]].set(low).at[spots[1]].set(top_value)


def block_levels(key, extent, split, low, largest):
    def one(axis_at, parts):
        heights = jax.random.uniform(jax.random.fold_in(jax.random.fold_in(key, 6), axis_at), (parts,), jnp.float32, low / len(split), largest / len(split))
        return jnp.repeat(jnp.exp(heights), extent[axis_at] // parts).reshape((-1,) + (1,) * (len(extent) - axis_at - 1))

    loudness = one(*split[0])
    for cut in split[1:]:
        loudness = loudness * one(*cut)
    return loudness


def bell_draw(own_key, shape, deviation, limit, split=(), dtype=jnp.bfloat16):
    values = deviation * jax.random.normal(own_key, shape, jnp.float32)
    if split:
        values = values * block_levels(own_key, shape, split, -0.22, 0.18)
    return jnp.clip(values, -limit, limit).astype(dtype)


def setup_inputs(seed: int = 0) -> dict:
    splits = jax.random.split(jax.random.key(seed), 4)
    state_field = bell_draw(splits[0], (GRIDS, NX, Q, Q, Q, Q, L), 1.0, 6.0, ((0, 4), (1, 8)), jnp.float32)
    levels = set_ends(jax.random.randint(splits[1], (GRIDS, 6), 1, 5), jax.random.fold_in(splits[1], 1), 1, 4).astype(jnp.int32)
    sign_bits = set_ends(jax.random.randint(splits[2], (GRIDS,), 0, 2), jax.random.fold_in(splits[2], 1), 0, 1).astype(jnp.int32)
    return {"state_field": state_field, "levels": levels, "sign_bits": sign_bits}


def hierarchize(values):
    points = values.shape[0]
    stride = 1
    while stride < points:
        blocks = values.reshape(points // (2 * stride), 2 * stride, -1)
        anchor = blocks[:, 0]
        right = jnp.roll(anchor, -1, 0)
        blocks = blocks.at[:, stride].add(-0.5 * (anchor + right))
        values = blocks.reshape(points, -1)
        stride = stride * 2
    return values


def dehierarchize(values):
    points = values.shape[0]
    stride = points // 2
    while stride >= 1:
        blocks = values.reshape(points // (2 * stride), 2 * stride, -1)
        anchor = blocks[:, 0]
        right = jnp.roll(anchor, -1, 0)
        blocks = blocks.at[:, stride].add(0.5 * (anchor + right))
        values = blocks.reshape(points, -1)
        stride = stride // 2
    return values


def level_depth(points):
    depth_max = points.bit_length() - 1
    position = np.arange(points)
    depth = np.full(points, depth_max)
    for power in range(1, depth_max + 1):
        depth = np.where(position % (2 ** power) == 0, depth_max - power, depth)
    return depth, depth_max


def advance(padded, diffuse, advect):
    centre = padded[1:-1]
    forward = padded[2:]
    backward = padded[:-2]
    result = centre + diffuse[0] * (forward - 2.0 * centre + backward) - advect[0] * (forward * forward - backward * backward) * 0.25
    for dimension in range(1, 6):
        forward = jnp.roll(centre, -1, dimension)
        backward = jnp.roll(centre, 1, dimension)
        result = result + diffuse[dimension] * (forward - 2.0 * centre + backward) - advect[dimension] * (forward * forward - backward * backward) * 0.25
    return result


def reference(state_field, levels, sign_bits):
    points = state_field.shape[1]
    depth_np, depth_max = level_depth(points)
    depth = jnp.asarray(depth_np, jnp.int32)

    def evolve_grid(item):
        values, level_row, sign_bit = item
        rates = jnp.exp2(level_row.astype(jnp.float32) - 4.0)
        diffuse = 0.08 * rates
        advect = 0.05 * rates
        for timestep in range(STEPS):
            padded = jnp.concatenate([values[-1:], values, values[:1]], 0)
            values = advance(padded, diffuse, advect)
        surplus = hierarchize(values.reshape(points, -1))
        sign_value = (2 * sign_bit - 1).astype(jnp.float32)
        return sign_value * surplus

    weighted = lax.map(evolve_grid, (state_field, levels, sign_bits))
    combined = jnp.sum(weighted, 0)

    def rebuild_grid(level_first):
        keep_mask = jnp.where(depth <= depth_max - 4 + level_first, 1.0, 0.0).astype(jnp.float32)
        rebuilt = dehierarchize(keep_mask[:, None] * combined)
        return rebuilt.reshape(state_field.shape[1:])

    return lax.map(rebuild_grid, levels[:, 0])
```

```python
import functools

import jax
import jax.numpy as jnp
from jax import lax
from jax.experimental import pallas as pl
from jax.experimental.pallas import tpu as pltpu
from jax.sharding import PartitionSpec as P

STEPS = 4
ALPHA = 0.08
BETA = 0.0125
LOADS = 4


def rate_of(level):
    return jnp.where(
        level >= 4, 1.0, jnp.where(level == 3, 0.5, jnp.where(level == 2, 0.25, 0.125))
    ).astype(jnp.float32)


def kernel(
    grids, tiles, X, B,
    levels_hbm, sign_hbm, x_ref, o_ref,
    levels_ref, sign_ref, raw, pa, ma, pb, mb, val, from_pair, part, from_far, comb,
    small_sem, load_sem, halo_send, halo_recv, pair_send, pair_recv, far_send, far_recv,
    back_send, back_recv, next_send, next_recv,
):
    H = STEPS
    g = lax.axis_index("grid")
    t = lax.axis_index("tile")
    core = g % 2
    pair = g + 1 - 2 * core
    right = (t + 1) % tiles
    left = (t + tiles - 1) % tiles
    far = grids // 2

    def to(grid_at, tile_at):
        return {"grid": grid_at, "tile": tile_at}

    def remote(src, dst, send, recv, where):
        return pltpu.make_async_remote_copy(
            src_ref=src, dst_ref=dst, send_sem=send, recv_sem=recv,
            device_id=where, device_id_type=pl.DeviceIdType.MESH,
        )

    piece = X // LOADS

    def load(i):
        return pltpu.make_async_copy(
            x_ref.at[pl.ds(i * piece, piece)], raw.at[pl.ds(H + i * piece, piece)], load_sem.at[i]
        )

    load_levels = pltpu.make_async_copy(levels_hbm, levels_ref, small_sem.at[0])
    load_sign = pltpu.make_async_copy(sign_hbm, sign_ref, small_sem.at[1])
    load_levels.start()
    load_sign.start()
    for i in range(LOADS):
        load(i).start()

    barrier = pltpu.get_barrier_semaphore()
    others = [to(g, left), to(g, right), to(pair, t)]
    others += [to((g + 2 * k) % grids, t) for k in range(1, far)]
    for other in others:
        pl.semaphore_signal(barrier, inc=1, device_id=other, device_id_type=pl.DeviceIdType.MESH)
    pl.semaphore_wait(barrier, len(others))

    def halo(side, k):
        return remote(
            x_ref.at[(1 - side) * (X - 1 - k) + side * k],
            raw.at[(1 - side) * (H - 1 - k) + side * (X + H + k)],
            halo_send.at[side, k], halo_recv.at[side, k],
            to(g, (t + 1 + side * (tiles - 2)) % tiles),
        )

    for k in range(H):
        halo(0, k).start()
    load_levels.wait()
    load_sign.wait()

    rates = [rate_of(levels_ref[0, d]) for d in range(6)]
    total = rates[0] + rates[1] + rates[2] + rates[3] + rates[4] + rates[5]
    centre = 1.0 / (2.0 * ALPHA) - total
    sign = (2 * sign_ref[0] - 1).astype(jnp.float32)

    blocks = 4
    sub = lax.broadcasted_iota(jnp.int32, (2, 8, 128), 1)
    low = sub < 4
    first = sub % 4 == 0
    last = sub % 4 == 3
    fine = blocks * blocks

    def split(u, p_ref, m_ref, layer, rows):
        bent = BETA * u
        p_ref[layer, rows] = u * (ALPHA - bent)
        m_ref[layer, rows] = u * (ALPHA + bent)

    def convert(layer):
        def body(i, carry):
            rows = pl.ds(pl.multiple_of(i * B, B), B)
            split(raw[layer, rows], pa, ma, layer, rows)
            return carry
        lax.fori_loop(0, blocks, body, 0, unroll=2)

    def swapped(v):
        return jnp.concatenate([v[1:2], v[0:1]], 0)

    def at_rows(i):
        return pl.ds(i * 2, 2)

    def stencil(p_ref, m_ref, layer, i):
        rows = at_rows(i)
        p = p_ref[layer, rows]
        m = m_ref[layer, rows]
        p5 = pltpu.roll(p, 127, 2)
        m5 = pltpu.roll(m, 1, 2)
        acc = centre * (p + m)
        acc += rates[0] * (p_ref[layer + 1, rows] + m_ref[layer - 1, rows])
        i1, i2 = i // blocks * blocks, i % blocks
        acc += rates[1] * (
            p_ref[layer, at_rows((i + blocks) % fine)]
            + m_ref[layer, at_rows((i + fine - blocks) % fine)]
        )
        acc += rates[2] * (
            p_ref[layer, at_rows(i1 + (i2 + 1) % blocks)]
            + m_ref[layer, at_rows(i1 + (i2 + blocks - 1) % blocks)]
        )
        ph = pltpu.roll(p, 4, 1)
        mh = pltpu.roll(m, 4, 1)
        acc += rates[3] * (jnp.where(low, ph, swapped(ph)) + jnp.where(low, swapped(mh), mh))
        p4 = pltpu.roll(jnp.where(first, ph, p), 7, 1)
        m4 = pltpu.roll(jnp.where(last, mh, m), 1, 1)
        acc += rates[4] * (p4 + m4)
        acc += rates[5] * (p5 + m5)
        return acc, rows

    state = [(pa, ma), (pb, mb)]

    def step(at, layer):
        src, dst = state[at % 2], state[(at + 1) % 2]
        for n in range(fine):
            acc, rows = stencil(*src, layer, n)
            if at == STEPS - 1:
                val[layer - H, rows] = sign * acc
            else:
                split(acc, *dst, layer, rows)

    half = B * blocks // 2
    mine = pl.ds(pl.multiple_of(core * half, half), half)
    theirs = pl.ds(pl.multiple_of((1 - core) * half, half), half)

    inner = X - 2 * H
    waves = X + 2 * H

    def place(n):
        past = n // inner
        ending = n // (inner + H)
        return n + (1 - past) * H + (past - ending) * (2 * inner + H - 1 - 2 * n - inner)

    def pair_copy(n):
        i = place(n)
        return remote(
            val.at[i, theirs], from_pair.at[i], pair_send.at[n], pair_recv.at[n], to(pair, t)
        )

    def far_copy(n, k):
        i = place(n)
        return remote(
            part.at[i], from_far.at[k - 1, i],
            far_send.at[k - 1, n], far_recv.at[k - 1, n], to((g + 2 * k) % grids, t),
        )

    def back_copy(n):
        own = comb.at[place(n), mine]
        return remote(own, own, back_send.at[n], back_recv.at[n], to(pair, t))

    def reduce_pair(n):
        pair_copy(n).wait_recv()
        i = place(n)
        part[i] = val[i, mine] + from_pair[i]
        for k in range(1, far):
            far_copy(n, k).start()

    def reduce_far(n):
        for k in range(1, far):
            far_copy(n, k).wait_recv()
        i = place(n)
        summed = part[i]
        for k in range(1, far):
            summed += from_far[k - 1, i]
        comb[i, mine] = summed
        back_copy(n).start()

    ahead = [1, 1, 2, 3, 6, 8, 10, 11]
    ahead = [min(n, X) for n in ahead]

    def done_before(w):
        count = 0
        for j, n in enumerate(ahead):
            more = n - (ahead[j - 1] if j else 0)
            count = count + more * jnp.minimum(jnp.maximum(w - (X + j) + 1, 0), 1)
        return count

    def wave(w, carry):
        ending = w // (X + H)
        leftward = w // X - ending
        at = (1 - leftward) * (w - H * ending) + leftward * (X - 1 - w)
        back = 1 - 2 * leftward

        @pl.when((w < X) & (w % piece == 0))
        def _():
            load(w // piece).wait()

        @pl.when(w >= X)
        def _():
            def finish(n, carry):
                reduce_far(n)
                return carry
            lax.fori_loop(done_before(w - 1), done_before(w), finish, 0)
            halo(ending, (w - X) % H).wait_recv()

        @pl.when(w == X + H - 2)
        def _():
            for k in range(H):
                halo(1, k).start()

        convert(at + H)
        for s in range(STEPS):
            @pl.when(w >= 2 * (s + 1))
            def _(s=s):
                step(s, at - back * (s + 1) + H)

        @pl.when(w >= 2 * H)
        def _():
            pair_copy(w - 2 * H).start()

        @pl.when(w >= 2 * H + 1)
        def _():
            reduce_pair(w - 2 * H - 1)
        return carry

    lax.fori_loop(0, waves, wave, 0)

    following = remote(comb.at[0, mine], comb.at[X, mine], next_send.at[0], next_recv.at[0], to(g, left))
    shared = remote(comb.at[X, mine], comb.at[X, mine], next_send.at[1], next_recv.at[1], to(pair, t))

    level = levels_ref[0, 0]
    reach = 8

    def nodes(base, rows):
        return comb[base, rows], comb[base + reach, rows]

    def rebuilt(base, rows, top):
        v = {0: comb[base, rows], reach: comb[base + reach, rows]}
        depth, gap = 2, reach // 2
        while gap >= 1:
            for i in range(gap, reach, 2 * gap):
                mean = 0.5 * (v[i - gap] + v[i + gap])
                if i < top:
                    v[i] = jnp.where(level >= depth, comb[base + i, rows], mean)
                else:
                    v[i] = mean
            depth, gap = depth + 1, gap // 2
        return v

    def write(base, top):
        def body(i, carry):
            rows = pl.ds(pl.multiple_of(i * 2, 2), 2)
            v = rebuilt(base, rows, top)
            for j in range(reach):
                o_ref[base + j, rows] = v[j]
            return carry
        lax.fori_loop(0, B * blocks // 2, body, 0, unroll=2)

    sums = ahead[-1]
    zero = inner + H - 1
    for n in range(sums, zero + 1):
        reduce_far(n)
    following.start()
    reduce_pair(X - 1)
    for n in range(zero + 1):
        back_copy(n).wait_recv()
    for q in range(X // reach - 1):
        write(q * reach, reach)
    for n in range(zero + 1, X - 1):
        reduce_far(n)
    following.wait_recv()
    shared.start()
    for n in range(zero + 1, X - 1):
        back_copy(n).wait_recv()
    shared.wait_recv()
    write(X - reach, reach - 1)
    reduce_far(X - 1)
    back_copy(X - 1).wait_recv()

    def tail(i, carry):
        rows = pl.ds(pl.multiple_of(i * B, B), B)
        o_ref[X - 1, rows] = jnp.where(level >= 4, comb[X - 1, rows], o_ref[X - 1, rows])
        return carry
    lax.fori_loop(0, blocks, tail, 0, unroll=2)

    for k in range(H):
        halo(0, k).wait_send()
        halo(1, k).wait_send()

    def drain(n, carry):
        pair_copy(n).wait_send()
        for k in range(1, far):
            far_copy(n, k).wait_send()
        back_copy(n).wait_send()
        return carry
    lax.fori_loop(0, X, drain, 0)
    following.wait_send()
    shared.wait_send()


def solution(mesh):
    grids, tiles = mesh.shape["grid"], mesh.shape["tile"]

    def on_device(state_field, levels, sign_bits):
        X = state_field.shape[1]
        L = state_field.shape[-1]
        V = state_field.size // (X * 8 * L)
        B = V // state_field.shape[2]
        H = STEPS
        far = grids // 2 - 1
        f32 = jnp.float32
        field = (V, 8, L)
        halved = (V // 2, 8, L)
        dma = pltpu.SemaphoreType.DMA
        state = pltpu.with_memory_space_constraint(state_field.reshape(X, *field), pltpu.HBM)
        levels = pltpu.with_memory_space_constraint(levels, pltpu.HBM)
        result = pl.pallas_call(
            functools.partial(kernel, grids, tiles, X, B),
            out_shape=jax.ShapeDtypeStruct((X, *field), f32),
            in_specs=[pl.BlockSpec(memory_space=pltpu.HBM)] * 3,
            out_specs=pl.BlockSpec(memory_space=pltpu.VMEM),
            scratch_shapes=[
                pltpu.SMEM(levels.shape, jnp.int32),
                pltpu.SMEM(sign_bits.shape, jnp.int32),
                pltpu.VMEM((X + 2 * H, *field), f32),
                pltpu.VMEM((X + 2 * H, *field), f32),
                pltpu.VMEM((X + 2 * H, *field), f32),
                pltpu.VMEM((X + 2 * H, *field), f32),
                pltpu.VMEM((X + 2 * H, *field), f32),
                pltpu.VMEM((X, *field), f32),
                pltpu.VMEM((X, *halved), f32),
                pltpu.VMEM((X, *halved), f32),
                pltpu.VMEM((far, X, *halved), f32),
                pltpu.VMEM((X + 1, *field), f32),
                dma((2,)),
                dma((LOADS,)),
                dma((2, H)),
                dma((2, H)),
                dma((X,)),
                dma((X,)),
                dma((far, X)),
                dma((far, X)),
                dma((X,)),
                dma((X,)),
                dma((2,)),
                dma((2,)),
            ],
            compiler_params=pltpu.CompilerParams(
                collective_id=0, has_side_effects=True, vmem_limit_bytes=48 * 1024 * 1024
            ),
        )(levels, sign_bits, state)
        return result.reshape(state_field.shape)

    placed = (P("grid", "tile", None, None, None, None, None), P("grid", None), P("grid"))
    return jax.shard_map(
        on_device,
        mesh=mesh,
        in_specs=placed,
        out_specs=P("grid", "tile", None, None, None, None, None),
        check_vma=False,
    )
```

```python
import functools

import jax
import jax.numpy as jnp
from jax import lax
from jax.experimental import pallas as pl
from jax.experimental.pallas import tpu as pltpu
from jax.sharding import PartitionSpec as P

STEPS = 4
ALPHA = 0.08
BETA = 0.0125
KAPPA = BETA / ALPHA
LOADS = 4


def rate_of(level):
    return jnp.where(
        level >= 4, 1.0, jnp.where(level == 3, 0.5, jnp.where(level == 2, 0.25, 0.125))
    ).astype(jnp.float32)


def kernel(
    grids, tiles, X, B,
    levels_hbm, sign_hbm, x_ref, o_ref,
    levels_ref, sign_ref, raw, pa, ma, pb, mb, rest, val, from_pair, part, from_far, comb,
    small_sem, load_sem, halo_send, halo_recv, pair_send, pair_recv, far_send, far_recv,
    back_send, back_recv, next_send, next_recv, credit,
):
    H = STEPS
    g = lax.axis_index("grid")
    t = lax.axis_index("tile")
    core = g % 2
    pair = g + 1 - 2 * core
    right = (t + 1) % tiles
    left = (t + tiles - 1) % tiles
    far = grids // 2

    def to(grid_at, tile_at):
        return {"grid": grid_at, "tile": tile_at}

    def remote(src, dst, send, recv, where):
        return pltpu.make_async_remote_copy(
            src_ref=src, dst_ref=dst, send_sem=send, recv_sem=recv,
            device_id=where, device_id_type=pl.DeviceIdType.MESH,
        )

    piece = X // LOADS

    def load(i):
        return pltpu.make_async_copy(
            x_ref.at[pl.ds(i * piece, piece)], raw.at[pl.ds(H + i * piece, piece)], load_sem.at[i]
        )

    load_levels = pltpu.make_async_copy(levels_hbm, levels_ref, small_sem.at[0])
    load_sign = pltpu.make_async_copy(sign_hbm, sign_ref, small_sem.at[1])
    load(0).start()
    load_levels.start()
    load_sign.start()
    barrier = pltpu.get_barrier_semaphore()

    def greet(other):
        pl.semaphore_signal(barrier, inc=1, device_id=other, device_id_type=pl.DeviceIdType.MESH)

    others = [to(g, left), to(pair, t)]
    others += [to((g + 2 * k) % grids, t) for k in range(1, far)]
    for other in others:
        greet(other)

    @pl.when(t < tiles - 1)
    def _():
        greet(to(g, right))

    def give_credit():
        pl.semaphore_signal(
            credit, inc=1, device_id=to(g, right), device_id_type=pl.DeviceIdType.MESH
        )

    for i in range(1, LOADS):
        load(i).start()

    def halo(side, k):
        return remote(
            x_ref.at[(1 - side) * (X - 1 - k) + side * k],
            raw.at[(1 - side) * (H - 1 - k) + side * (X + H + k)],
            halo_send.at[side], halo_recv.at[side, k],
            to(g, (t + 1 + side * (tiles - 2)) % tiles),
        )

    blocks = 4
    sub = lax.broadcasted_iota(jnp.int32, (2, 8, 128), 1)
    low = sub < 4
    first = sub % 4 == 0
    last = sub % 4 == 3
    fine = blocks * blocks

    def split(v, p_ref, m_ref, layer, rows):
        square = v * v
        p_ref[layer, rows] = v - square
        m_ref[layer, rows] = v + square

    def convert(layer):
        for i in range(blocks):
            rows = pl.ds(i * B, B)
            split(KAPPA * raw[layer, rows], pa, ma, layer, rows)

    def convert_from(lo, hi):
        def body(i, carry):
            convert(i + H)
            return carry
        lax.fori_loop(lo, hi, body, 0)

    load(0).wait()
    convert_from(0, piece)
    pl.semaphore_wait(barrier, len(others) + jnp.minimum(t, 1))

    @pl.when(t == tiles - 1)
    def _():
        give_credit()

    for k in range(H):
        halo(0, k).start()

    odd = t % 2

    @pl.when(odd == 1)
    def _():
        for k in range(H):
            halo(1, k).start()

    for lo in range(piece, 2 * H + 1, piece):
        load(lo // piece).wait()
        convert_from(lo, min(lo + piece, 2 * H + 1))
    load_levels.wait()
    load_sign.wait()

    rates = [ALPHA * rate_of(levels_ref[0, d]) for d in range(6)]
    total = rates[0] + rates[1] + rates[2] + rates[3] + rates[4] + rates[5]
    centre = 0.5 - total
    sign = (2 * sign_ref[0] - 1).astype(jnp.float32) * (1.0 / KAPPA)

    def swapped(v):
        return jnp.concatenate([v[1:2], v[0:1]], 0)

    def at_rows(i):
        return pl.ds(i * 2, 2)

    def stencil(p_ref, m_ref, layer, i, upper):
        rows = at_rows(i)
        p = p_ref[layer, rows]
        m = m_ref[layer, rows]
        p5 = pltpu.roll(p, 127, 2)
        m5 = pltpu.roll(m, 1, 2)
        acc = centre * (p + m)
        if upper:
            acc += rates[0] * (p_ref[layer + 1, rows] + m_ref[layer - 1, rows])
        else:
            acc += rates[0] * m_ref[layer - 1, rows]
        i1, i2 = i // blocks * blocks, i % blocks
        acc += rates[1] * (
            p_ref[layer, at_rows((i + blocks) % fine)]
            + m_ref[layer, at_rows((i + fine - blocks) % fine)]
        )
        acc += rates[2] * (
            p_ref[layer, at_rows(i1 + (i2 + 1) % blocks)]
            + m_ref[layer, at_rows(i1 + (i2 + blocks - 1) % blocks)]
        )
        ph = pltpu.roll(p, 4, 1)
        mh = pltpu.roll(m, 4, 1)
        acc += rates[3] * (jnp.where(low, ph, swapped(ph)) + jnp.where(low, swapped(mh), mh))
        p4 = pltpu.roll(jnp.where(first, ph, p), 7, 1)
        m4 = pltpu.roll(jnp.where(last, mh, m), 1, 1)
        acc += rates[4] * (p4 + m4)
        acc += rates[5] * (p5 + m5)
        return acc, rows

    state = [(pa, ma), (pb, mb)]

    def step(at, layer):
        src, dst = state[at % 2], state[(at + 1) % 2]
        for n in range(fine):
            acc, rows = stencil(*src, layer, n, True)
            if at == STEPS - 1:
                val[layer - H, rows] = sign * acc
            else:
                split(acc, *dst, layer, rows)

    def partly(at, layer):
        for n in range(fine):
            acc, rows = stencil(*state[at % 2], layer, n, False)
            rest[at, rows] = acc

    half = B * blocks // 2
    mine = pl.ds(pl.multiple_of(core * half, half), half)
    theirs = pl.ds(pl.multiple_of((1 - core) * half, half), half)

    inner = X - 2 * H

    def place(n):
        past = n // inner
        ending = n // (inner + H)
        return n + (1 - past) * H + (past - ending) * (2 * inner + H - 1 - 2 * n - inner)

    def pair_copy(n):
        i = place(n)
        return remote(val.at[i, theirs], from_pair.at[i], pair_send.at[0], pair_recv.at[n], to(pair, t))

    def far_copy(n, k):
        i = place(n)
        return remote(
            part.at[i], from_far.at[k - 1, i],
            far_send.at[k - 1], far_recv.at[k - 1, n], to((g + 2 * k) % grids, t),
        )

    def back_copy(n):
        own = comb.at[place(n), mine]
        return remote(own, own, back_send.at[0], back_recv.at[n], to(pair, t))

    def reduce_pair(n):
        pair_copy(n).wait_recv()
        i = place(n)
        part[i] = val[i, mine] + from_pair[i]
        for k in range(1, far):
            far_copy(n, k).start()

    def reduce_far(n):
        for k in range(1, far):
            far_copy(n, k).wait_recv()
        i = place(n)
        summed = part[i]
        for k in range(1, far):
            summed += from_far[k - 1, i]
        comb[i, mine] = summed
        back_copy(n).start()

    ahead = [min(n, X) for n in (2, 2, 3, 5, 7, 9, 10)]

    def done_before(j):
        count = 0
        for i, n in enumerate(ahead):
            more = n - (ahead[i - 1] if i else 0)
            count = count + more * jnp.minimum(jnp.maximum(j - i + 1, 0), 1)
        return count

    def finish_far(lo, hi):
        def body(n, carry):
            reduce_far(n)
            return carry
        lax.fori_loop(lo, hi, body, 0)

    for s in range(STEPS):
        def body(i, carry, s=s):
            step(s, i + H)
            return carry
        lax.fori_loop(s + 1, 2 * H - s, body, 0)
    pair_copy(0).start()

    def wave(n, carry):
        ending = n // (inner + H)
        leftward = n // inner - ending
        w = n + 2 * H
        at = (1 - leftward) * (w - H * ending) + leftward * (X - 1 - w)
        back = 1 - 2 * leftward

        @pl.when((n < inner) & (w % piece == 0))
        def _():
            load(w // piece).wait()

        @pl.when(n >= inner + H)
        def _():
            reduce_pair(n - 1)

        @pl.when(n >= inner)
        def _():
            j = n - inner
            more = jnp.maximum(1 - t, 0) * ahead[3]
            finish_far(
                jnp.maximum(done_before(j - 1), more * jnp.minimum(j // 3, 1)),
                jnp.maximum(done_before(j), more * jnp.minimum(j // 2, 1)),
            )

        @pl.when((odd == 0) & (n == inner + 2))
        def _():
            pl.semaphore_wait(credit, 1)
            for k in range(H):
                halo(1, k).start()

        @pl.when((n >= inner) & ((odd == 0) | (t == tiles - 1) | (n != inner + 2)))
        def _():
            halo(ending, (n - inner) % H).wait_recv()

        @pl.when((odd == 1) & (t < tiles - 1) & (n == inner + 1))
        def _():
            halo(ending, 2).wait_recv()
            give_credit()

        convert(at + H)
        for s in range(STEPS):
            step(s, at - back * (s + 1) + H)
        pair_copy(n).start()

        @pl.when(n < inner + H)
        def _():
            reduce_pair(n - 1)
        return carry

    lax.fori_loop(1, X - 1, wave, 0)

    end = X + H - 1
    for s in range(STEPS):
        partly(s, end - 1 - s + H)
    reduce_pair(X - 2)
    zero = inner + H - 1
    finish_far(ahead[-1], zero + 1)
    following = remote(comb.at[0, mine], comb.at[X, mine], next_send.at[0], next_recv.at[0], to(g, left))
    following.start()
    halo(1, H - 1).wait_recv()
    for i in range(blocks):
        rows = pl.ds(i * B, B)
        v = KAPPA * raw[end + H, rows]
        for s in range(STEPS):
            acc = rest[s, rows] + rates[0] * (v - v * v)
            if s == STEPS - 1:
                val[X - 1, rows] = sign * acc
            v = acc
    pair_copy(X - 1).start()

    shared = remote(comb.at[X, mine], comb.at[X, mine], next_send.at[1], next_recv.at[1], to(pair, t))

    level = levels_ref[0, 0]
    reach = 8

    def rebuilt(base, rows, top):
        v = {0: comb[base, rows], reach: comb[base + reach, rows]}
        depth, gap = 2, reach // 2
        while gap >= 1:
            for i in range(gap, reach, 2 * gap):
                mean = 0.5 * (v[i - gap] + v[i + gap])
                v[i] = jnp.where(level >= depth, comb[base + i, rows], mean) if i < top else mean
            depth, gap = depth + 1, gap // 2
        return v

    def write(base, top):
        def body(i, carry):
            rows = pl.ds(pl.multiple_of(i * 2, 2), 2)
            v = rebuilt(base, rows, top)
            for j in range(reach):
                o_ref[base + j, rows] = v[j]
            return carry
        lax.fori_loop(0, B * blocks // 2, body, 0, unroll=2)

    for n in range(zero + 1):
        back_copy(n).wait_recv()
    for q in range(X // reach - 1):
        write(q * reach, reach)
    reduce_pair(X - 1)
    for side in range(2):
        whole = raw.at[pl.ds(0, H)]
        remote(whole, whole, halo_send.at[side], halo_recv.at[side, 0], to(g, left)).wait_send()
    finish_far(zero + 1, X - 1)
    following.wait_recv()
    shared.start()
    reduce_far(X - 1)
    for n in range(zero + 1, X - 1):
        back_copy(n).wait_recv()
    shared.wait_recv()
    write(X - reach, reach - 1)
    following.wait_send()
    remote(part, part, pair_send.at[0], pair_recv.at[0], to(pair, t)).wait_send()
    shared.wait_send()
    back_copy(X - 1).wait_recv()
    for i in range(blocks):
        rows = pl.ds(i * B, B)
        o_ref[X - 1, rows] = jnp.where(level >= 4, comb[X - 1, rows], o_ref[X - 1, rows])
    for k in range(1, far):
        remote(part, part, far_send.at[k - 1], far_recv.at[k - 1, 0], to(pair, t)).wait_send()
    remote(part, part, back_send.at[0], back_recv.at[0], to(pair, t)).wait_send()


def solution(mesh):
    grids, tiles = mesh.shape["grid"], mesh.shape["tile"]

    def on_device(state_field, levels, sign_bits):
        X = state_field.shape[1]
        L = state_field.shape[-1]
        V = state_field.size // (X * 8 * L)
        B = V // state_field.shape[2]
        H = STEPS
        far = grids // 2 - 1
        f32 = jnp.float32
        field = (V, 8, L)
        halved = (V // 2, 8, L)
        dma = pltpu.SemaphoreType.DMA
        state = pltpu.with_memory_space_constraint(state_field.reshape(X, *field), pltpu.HBM)
        levels = pltpu.with_memory_space_constraint(levels, pltpu.HBM)
        result = pl.pallas_call(
            functools.partial(kernel, grids, tiles, X, B),
            out_shape=jax.ShapeDtypeStruct((X, *field), f32),
            in_specs=[pl.BlockSpec(memory_space=pltpu.HBM)] * 3,
            out_specs=pl.BlockSpec(memory_space=pltpu.VMEM),
            scratch_shapes=[
                pltpu.SMEM(levels.shape, jnp.int32),
                pltpu.SMEM(sign_bits.shape, jnp.int32),
                pltpu.VMEM((X + 2 * H, *field), f32),
                pltpu.VMEM((X + 2 * H, *field), f32),
                pltpu.VMEM((X + 2 * H, *field), f32),
                pltpu.VMEM((X + 2 * H, *field), f32),
                pltpu.VMEM((X + 2 * H, *field), f32),
                pltpu.VMEM((H, *field), f32),
                pltpu.VMEM((X, *field), f32),
                pltpu.VMEM((X, *halved), f32),
                pltpu.VMEM((X, *halved), f32),
                pltpu.VMEM((far, X, *halved), f32),
                pltpu.VMEM((X + 1, *field), f32),
                dma((2,)),
                dma((LOADS,)),
                dma((2,)),
                dma((2, H)),
                dma((1,)),
                dma((X,)),
                dma((far,)),
                dma((far, X)),
                dma((1,)),
                dma((X,)),
                dma((2,)),
                dma((2,)),
                pltpu.SemaphoreType.REGULAR,
            ],
            compiler_params=pltpu.CompilerParams(
                collective_id=0, has_side_effects=True, vmem_limit_bytes=48 * 1024 * 1024
            ),
        )(levels, sign_bits, state)
        return result.reshape(state_field.shape)

    placed = (P("grid", "tile", None, None, None, None, None), P("grid", None), P("grid"))
    return jax.shard_map(
        on_device,
        mesh=mesh,
        in_specs=placed,
        out_specs=P("grid", "tile", None, None, None, None, None),
        check_vma=False,
    )
```

```python
import functools

import jax
import jax.numpy as jnp
from jax import lax
from jax.experimental import pallas as pl
from jax.experimental.pallas import tpu as pltpu
from jax.sharding import PartitionSpec as P

STEPS = 4
ALPHA = 0.08
BETA = 0.0125
KAPPA = BETA / ALPHA
LOADS = 4


def rate_of(level):
    return jnp.where(
        level >= 4, 1.0, jnp.where(level == 3, 0.5, jnp.where(level == 2, 0.25, 0.125))
    ).astype(jnp.float32)


def kernel(
    grids, tiles, X, B,
    levels_hbm, sign_hbm, x_ref, o_ref,
    levels_ref, sign_ref, raw, pa, ma, pb, mb, rest, val, from_pair, part, from_far, comb,
    small_sem, load_sem, halo_send, halo_recv, pair_send, pair_recv, far_send, far_recv,
    back_send, back_recv, next_send, next_recv, credit, met,
):
    H = STEPS
    g = lax.axis_index("grid")
    t = lax.axis_index("tile")
    core = g % 2
    pair = g + 1 - 2 * core
    right = (t + 1) % tiles
    left = (t + tiles - 1) % tiles
    far = grids // 2

    def to(grid_at, tile_at):
        return {"grid": grid_at, "tile": tile_at}

    def remote(src, dst, send, recv, where):
        return pltpu.make_async_remote_copy(
            src_ref=src, dst_ref=dst, send_sem=send, recv_sem=recv,
            device_id=where, device_id_type=pl.DeviceIdType.MESH,
        )

    piece = X // LOADS

    def load(i):
        return pltpu.make_async_copy(
            x_ref.at[pl.ds(i * piece, piece)], raw.at[pl.ds(H + i * piece, piece)], load_sem.at[i]
        )

    load_levels = pltpu.make_async_copy(levels_hbm, levels_ref, small_sem.at[0])
    load_sign = pltpu.make_async_copy(sign_hbm, sign_ref, small_sem.at[1])
    load(0).start()
    load_levels.start()
    load_sign.start()
    barrier = pltpu.get_barrier_semaphore()

    def greet(other):
        pl.semaphore_signal(barrier, inc=1, device_id=other, device_id_type=pl.DeviceIdType.MESH)

    others = [to(g, left), to(pair, t)]
    others += [to((g + 2 * k) % grids, t) for k in range(1, far)]
    for other in others:
        greet(other)

    @pl.when(t < tiles - 1)
    def _():
        greet(to(g, right))

    def give_credit():
        pl.semaphore_signal(
            credit, inc=1, device_id=to(g, right), device_id_type=pl.DeviceIdType.MESH
        )

    for i in range(1, LOADS):
        load(i).start()

    def halo(side, k):
        return remote(
            x_ref.at[(1 - side) * (X - 1 - k) + side * k],
            raw.at[(1 - side) * (H - 1 - k) + side * (X + H + k)],
            halo_send.at[side], halo_recv.at[side * H + k],
            to(g, (t + 1 + side * (tiles - 2)) % tiles),
        )

    blocks = 4

    def last_halo(q):
        rows = pl.ds(q * B, B)
        return remote(
            x_ref.at[H - 1, rows], raw.at[X + 2 * H - 1, rows],
            halo_send.at[1], halo_recv.at[2 * H - 1 + q], to(g, left),
        )

    part_at = B

    def third_halo(q):
        rows = pl.ds(q * part_at, part_at - q * (2 * part_at - blocks * B))
        return remote(
            x_ref.at[X - 3, rows], raw.at[H - 3, rows],
            halo_send.at[0], halo_recv.at[2 + q * (2 * H + 1)], to(g, right),
        )

    def start_left():
        for k in range(2):
            halo(0, k).start()
        for q in range(2):
            third_halo(q).start()
        for k in range(3, H):
            halo(0, k).start()

    def start_right():
        for k in range(H - 1):
            halo(1, k).start()
        for q in range(blocks):
            last_halo(q).start()

    sub = lax.broadcasted_iota(jnp.int32, (2, 8, 128), 1)
    low = sub < 4
    first = sub % 4 == 0
    last = sub % 4 == 3
    fine = blocks * blocks

    def split(v, p_ref, m_ref, layer, rows):
        square = v * v
        p_ref[layer, rows] = v - square
        m_ref[layer, rows] = v + square

    def convert(layer):
        for i in range(blocks):
            rows = pl.ds(i * B, B)
            split(KAPPA * raw[layer, rows], pa, ma, layer, rows)

    def convert_from(lo, hi):
        def body(i, carry):
            convert(i + H)
            return carry
        lax.fori_loop(lo, hi, body, 0)

    load(0).wait()
    convert_from(0, piece)
    pl.semaphore_wait(barrier, len(others) + jnp.minimum(t, 1))

    @pl.when(t == tiles - 1)
    def _():
        give_credit()

    start_left()

    odd = t % 2

    @pl.when(odd == 1)
    def _():
        start_right()

    for lo in range(piece, 2 * H + 1, piece):
        load(lo // piece).wait()
        convert_from(lo, min(lo + piece, 2 * H + 1))
    load_levels.wait()
    load_sign.wait()

    rates = [ALPHA * rate_of(levels_ref[0, d]) for d in range(6)]
    total = rates[0] + rates[1] + rates[2] + rates[3] + rates[4] + rates[5]
    centre = 0.5 - total
    sign = (2 * sign_ref[0] - 1).astype(jnp.float32) * (1.0 / KAPPA)

    def swapped(v):
        return jnp.concatenate([v[1:2], v[0:1]], 0)

    def at_rows(i):
        return pl.ds(i * 2, 2)

    def stencil(p_ref, m_ref, layer, i, upper):
        rows = at_rows(i)
        p = p_ref[layer, rows]
        m = m_ref[layer, rows]
        p5 = pltpu.roll(p, 127, 2)
        m5 = pltpu.roll(m, 1, 2)
        acc = centre * (p + m)
        if upper:
            acc += rates[0] * (p_ref[layer + 1, rows] + m_ref[layer - 1, rows])
        else:
            acc += rates[0] * m_ref[layer - 1, rows]
        i1, i2 = i // blocks * blocks, i % blocks
        acc += rates[1] * (
            p_ref[layer, at_rows((i + blocks) % fine)]
            + m_ref[layer, at_rows((i + fine - blocks) % fine)]
        )
        acc += rates[2] * (
            p_ref[layer, at_rows(i1 + (i2 + 1) % blocks)]
            + m_ref[layer, at_rows(i1 + (i2 + blocks - 1) % blocks)]
        )
        ph = pltpu.roll(p, 4, 1)
        mh = pltpu.roll(m, 4, 1)
        acc += rates[3] * (jnp.where(low, ph, swapped(ph)) + jnp.where(low, swapped(mh), mh))
        p4 = pltpu.roll(jnp.where(first, ph, p), 7, 1)
        m4 = pltpu.roll(jnp.where(last, mh, m), 1, 1)
        acc += rates[4] * (p4 + m4)
        acc += rates[5] * (p5 + m5)
        return acc, rows

    state = [(pa, ma), (pb, mb)]

    def step(at, layer):
        src, dst = state[at % 2], state[(at + 1) % 2]
        for n in range(fine):
            acc, rows = stencil(*src, layer, n, True)
            if at == STEPS - 1:
                val[layer - H, rows] = sign * acc
            else:
                split(acc, *dst, layer, rows)

    def partly(at, layer):
        for n in range(fine):
            acc, rows = stencil(*state[at % 2], layer, n, False)
            rest[at, rows] = acc

    half = B * blocks // 2
    mine = pl.ds(pl.multiple_of(core * half, half), half)
    theirs = pl.ds(pl.multiple_of((1 - core) * half, half), half)

    inner = X - 2 * H

    def place(n):
        past = jnp.minimum(n // inner, 1)
        done = jnp.minimum(n // (X - H), 1)
        return n + (1 - past) * H + (past - done) * (X - H - 1 - 2 * n)

    def pair_copy(n):
        i = place(n)
        return remote(
            val.at[i, theirs], from_pair.at[i], pair_send.at[0], pair_recv.at[n % 4], to(pair, t)
        )

    def far_copy(n, k):
        i = place(n)
        return remote(
            part.at[i], from_far.at[k - 1, i],
            far_send.at[k - 1], far_recv.at[k - 1, n], to((g + 2 * k) % grids, t),
        )

    def back_copy(n):
        own = comb.at[place(n), mine]
        group = jnp.minimum(n // (X - H), 1)
        return remote(own, own, back_send.at[0], back_recv.at[group], to(pair, t))

    def backs_done(group, count):
        some = part.at[pl.ds(0, count)]
        remote(some, some, back_send.at[0], back_recv.at[group], to(pair, t)).wait_recv()

    def reduce_pair(n):
        pair_copy(n).wait_recv()
        i = place(n)
        part[i] = val[i, mine] + from_pair[i]
        for k in range(1, far):
            far_copy(n, k).start()

    def reduce_far(n):
        for k in range(1, far):
            far_copy(n, k).wait_recv()
        i = place(n)
        summed = part[i]
        for k in range(1, far):
            summed += from_far[k - 1, i]
        comb[i, mine] = summed
        back_copy(n).start()

    small = B // 2

    def own_rows(q):
        return pl.ds(pl.multiple_of(q * B + core * small, small), small)

    def other_rows(q):
        return pl.ds(pl.multiple_of(q * B + (1 - core) * small, small), small)

    def kept(q):
        return pl.ds(q * small, small)

    def last_pair(q):
        return remote(
            val.at[X - 1, other_rows(q)], from_pair.at[X - 1, kept(q)],
            pair_send.at[0], pair_recv.at[4 + q], to(pair, t),
        )

    def last_far(q, k):
        return remote(
            part.at[X - 1, kept(q)], from_far.at[k - 1, X - 1, kept(q)],
            far_send.at[k - 1], far_recv.at[k - 1, X - 1 + q], to((g + 2 * k) % grids, t),
        )

    def last_back(q):
        own = comb.at[X - 1, own_rows(q)]
        return remote(own, own, back_send.at[0], back_recv.at[2], to(pair, t))

    ahead = [2, 2, 3, 5, 7, 9, 10]
    held = 5

    def done_before(j):
        count = 0
        for i, n in enumerate(ahead):
            more = n - (ahead[i - 1] if i else 0)
            count = count + more * jnp.minimum(jnp.maximum(j - i + 1, 0), 1)
        return jnp.maximum(count, jnp.maximum(1 - t, 0) * held * jnp.minimum(jnp.maximum(j - 1, 0), 1))

    def finish_far(lo, hi):
        def body(n, carry):
            reduce_far(n)
            return carry
        lax.fori_loop(lo, hi, body, 0)

    following = remote(comb.at[0, mine], comb.at[X, mine], next_send.at[0], next_recv.at[0], to(g, left))
    shared = remote(comb.at[X, mine], comb.at[X, mine], next_send.at[1], next_recv.at[1], to(pair, t))

    for s in range(STEPS):
        def body(i, carry, s=s):
            step(s, i + H)
            return carry
        lax.fori_loop(s + 1, 2 * H - s, body, 0)
    pair_copy(0).start()

    def wave(n, carry):
        leftward = n // inner
        back = 1 - 2 * leftward
        at = (1 - leftward) * (n + 2 * H) + leftward * (inner - 1 - n)
        j = n - inner

        @pl.when((leftward == 0) & (at % piece == 0))
        def _():
            load(at // piece).wait()

        @pl.when(leftward == 1)
        def _():
            finish_far(done_before(j - 1), done_before(j))

        @pl.when((t == 0) & (j == 2))
        def _():
            pl.semaphore_wait(credit, 1)
            start_right()

        @pl.when((leftward == 1) & (j != 2))
        def _():
            halo(0, j).wait_recv()

        paced = (odd == 1) & (t < tiles - 1)

        @pl.when((j == 2) & ((odd == 0) | (t == tiles - 1)))
        def _():
            third_halo(0).wait_recv()

        @pl.when(j == 2)
        def _():
            third_halo(1).wait_recv()

        @pl.when(paced & (j == 0))
        def _():
            third_halo(0).wait_recv()
            pl.semaphore_signal(
                met, inc=1, device_id=to(pair, t), device_id_type=pl.DeviceIdType.MESH
            )
            pl.semaphore_wait(met, 1)
            give_credit()

        convert(at + H)
        for s in range(STEPS):
            step(s, at - back * (s + 1) + H)
        pair_copy(n).start()

        @pl.when((odd == 0) & (t > 0) & (j == 1))
        def _():
            pl.semaphore_wait(credit, 1)
            start_right()

        reduce_pair(n - 1)
        return carry

    lax.fori_loop(1, X - H, wave, 0)

    def prepare(n):
        for s in range(STEPS):
            partly(s, n + 2 * H - 1 - s)
        reduce_pair(n - 1)

    def complete(n, q, keep):
        rows = pl.ds(q * B, B)
        v = KAPPA * raw[n + 2 * H, rows]
        for s in range(STEPS):
            square = v * v
            p = v - square
            if keep:
                p_ref, m_ref = state[s % 2]
                p_ref[n + 2 * H - s, rows] = p
                m_ref[n + 2 * H - s, rows] = v + square
            v = rest[s, rows] + rates[0] * p
        val[n, rows] = sign * v

    def ending(n, carry):
        j = n - inner
        prepare(n)
        finish_far(done_before(j - 1), done_before(j))
        halo(1, n - (X - H)).wait_recv()
        for q in range(blocks):
            complete(n, q, True)
        pair_copy(n).start()
        return carry

    lax.fori_loop(X - H, X - 1, ending, 0)
    finish_far(ahead[-1], X - H)
    following.start()
    prepare(X - 1)
    for q in range(blocks):
        last_halo(q).wait_recv()
        complete(X - 1, q, False)
        last_pair(q).start()

    level = levels_ref[0, 0]
    reach = 8

    def rebuilt(base, rows, top):
        v = {0: comb[base, rows], reach: comb[base + reach, rows]}
        depth, gap = 2, reach // 2
        while gap >= 1:
            for i in range(gap, reach, 2 * gap):
                mean = 0.5 * (v[i - gap] + v[i + gap])
                v[i] = jnp.where(level >= depth, comb[base + i, rows], mean) if i < top else mean
            depth, gap = depth + 1, gap // 2
        return v

    def write(base, top):
        def body(i, carry):
            rows = pl.ds(pl.multiple_of(i * 2, 2), 2)
            v = rebuilt(base, rows, top)
            for j in range(reach):
                o_ref[base + j, rows] = v[j]
            return carry
        lax.fori_loop(0, B * blocks // 2, body, 0, unroll=2)

    backs_done(0, X - H)
    for q in range(X // reach - 1):
        write(q * reach, reach)
    for q in range(blocks):
        last_pair(q).wait_recv()
        part[X - 1, kept(q)] = val[X - 1, own_rows(q)] + from_pair[X - 1, kept(q)]
        for k in range(1, far):
            last_far(q, k).start()
    following.wait_recv()
    shared.start()
    finish_far(X - H, X - 1)
    for q in range(blocks):
        for k in range(1, far):
            last_far(q, k).wait_recv()
        summed = part[X - 1, kept(q)]
        for k in range(1, far):
            summed += from_far[k - 1, X - 1, kept(q)]
        comb[X - 1, own_rows(q)] = summed
        last_back(q).start()
    for side in range(2):
        whole = raw.at[pl.ds(0, H)]
        remote(whole, whole, halo_send.at[side], halo_recv.at[0], to(g, left)).wait_send()
    backs_done(1, H - 1)
    shared.wait_recv()
    write(X - reach, reach - 1)
    following.wait_send()
    shared.wait_send()
    remote(part, part, pair_send.at[0], pair_recv.at[0], to(pair, t)).wait_send()
    backs_done(2, 1)
    for i in range(blocks):
        rows = pl.ds(i * B, B)
        o_ref[X - 1, rows] = jnp.where(level >= 4, comb[X - 1, rows], o_ref[X - 1, rows])
    for k in range(1, far):
        remote(part, part, far_send.at[k - 1], far_recv.at[k - 1, 0], to(pair, t)).wait_send()
    remote(part, part, back_send.at[0], back_recv.at[0], to(pair, t)).wait_send()


def solution(mesh):
    grids, tiles = mesh.shape["grid"], mesh.shape["tile"]

    def on_device(state_field, levels, sign_bits):
        X = state_field.shape[1]
        L = state_field.shape[-1]
        V = state_field.size // (X * 8 * L)
        B = V // state_field.shape[2]
        H = STEPS
        far = grids // 2 - 1
        f32 = jnp.float32
        field = (V, 8, L)
        halved = (V // 2, 8, L)
        dma = pltpu.SemaphoreType.DMA
        state = pltpu.with_memory_space_constraint(state_field.reshape(X, *field), pltpu.HBM)
        levels = pltpu.with_memory_space_constraint(levels, pltpu.HBM)
        result = pl.pallas_call(
            functools.partial(kernel, grids, tiles, X, B),
            out_shape=jax.ShapeDtypeStruct((X, *field), f32),
            in_specs=[pl.BlockSpec(memory_space=pltpu.HBM)] * 3,
            out_specs=pl.BlockSpec(memory_space=pltpu.VMEM),
            scratch_shapes=[
                pltpu.SMEM(levels.shape, jnp.int32),
                pltpu.SMEM(sign_bits.shape, jnp.int32),
                pltpu.VMEM((X + 2 * H, *field), f32),
                pltpu.VMEM((X + 2 * H, *field), f32),
                pltpu.VMEM((X + 2 * H, *field), f32),
                pltpu.VMEM((X + 2 * H, *field), f32),
                pltpu.VMEM((X + 2 * H, *field), f32),
                pltpu.VMEM((H, *field), f32),
                pltpu.VMEM((X, *field), f32),
                pltpu.VMEM((X, *halved), f32),
                pltpu.VMEM((X, *halved), f32),
                pltpu.VMEM((far, X, *halved), f32),
                pltpu.VMEM((X + 1, *field), f32),
                dma((2,)),
                dma((LOADS,)),
                dma((2,)),
                dma((2 * H + 4,)),
                dma((1,)),
                dma((8,)),
                dma((far,)),
                dma((far, X + 3)),
                dma((1,)),
                dma((3,)),
                dma((2,)),
                dma((2,)),
                pltpu.SemaphoreType.REGULAR,
                pltpu.SemaphoreType.REGULAR,
            ],
            compiler_params=pltpu.CompilerParams(
                collective_id=0, has_side_effects=True, vmem_limit_bytes=48 * 1024 * 1024
            ),
        )(levels, sign_bits, state)
        return result.reshape(state_field.shape)

    placed = (P("grid", "tile", None, None, None, None, None), P("grid", None), P("grid"))
    return jax.shard_map(
        on_device,
        mesh=mesh,
        in_specs=placed,
        out_specs=P("grid", "tile", None, None, None, None, None),
        check_vma=False,
    )
```

```python
import functools

import jax
import jax.numpy as jnp
from jax import lax
from jax.experimental import pallas as pl
from jax.experimental.pallas import tpu as pltpu
from jax.sharding import PartitionSpec as P

STEPS = 4
ALPHA = 0.08
BETA = 0.0125
KAPPA = BETA / ALPHA
LOADS = 4


def rate_of(level):
    return jnp.where(
        level >= 4, 1.0, jnp.where(level == 3, 0.5, jnp.where(level == 2, 0.25, 0.125))
    ).astype(jnp.float32)


def kernel(
    grids, tiles, X, B,
    levels_hbm, sign_hbm, x_ref, o_ref,
    levels_ref, sign_ref, raw, pa, ma, pb, mb, rest, val, from_pair, part, from_far, comb,
    small_sem, load_sem, halo_send, halo_recv, pair_send, pair_recv, far_send, far_recv,
    back_send, back_recv, next_recv, credit, met,
):
    H = STEPS
    g = lax.axis_index("grid")
    t = lax.axis_index("tile")
    core = g % 2
    pair = g + 1 - 2 * core
    right = (t + 1) % tiles
    left = (t + tiles - 1) % tiles
    far = grids // 2

    def to(grid_at, tile_at):
        return {"grid": grid_at, "tile": tile_at}

    def remote(src, dst, send, recv, where):
        return pltpu.make_async_remote_copy(
            src_ref=src, dst_ref=dst, send_sem=send, recv_sem=recv,
            device_id=where, device_id_type=pl.DeviceIdType.MESH,
        )

    piece = X // LOADS

    def load(i):
        return pltpu.make_async_copy(
            x_ref.at[pl.ds(i * piece, piece)], raw.at[pl.ds(H + i * piece, piece)], load_sem.at[i]
        )

    load_levels = pltpu.make_async_copy(levels_hbm, levels_ref, small_sem.at[0])
    load_sign = pltpu.make_async_copy(sign_hbm, sign_ref, small_sem.at[1])
    load(0).start()
    load_levels.start()
    load_sign.start()
    barrier = pltpu.get_barrier_semaphore()

    def greet(other):
        pl.semaphore_signal(barrier, inc=1, device_id=other, device_id_type=pl.DeviceIdType.MESH)

    others = [to(g, left), to(pair, t)]
    others += [to((g + 2 * k) % grids, t) for k in range(1, far)]
    for other in others:
        greet(other)

    @pl.when(t < tiles - 1)
    def _():
        greet(to(g, right))

    def give_credit():
        pl.semaphore_signal(
            credit, inc=1, device_id=to(g, right), device_id_type=pl.DeviceIdType.MESH
        )

    for i in range(1, LOADS):
        load(i).start()

    def halo(side, k):
        return remote(
            x_ref.at[(1 - side) * (X - 1 - k) + side * k],
            raw.at[(1 - side) * (H - 1 - k) + side * (X + H + k)],
            halo_send.at[0], halo_recv.at[side * H + k],
            to(g, (t + 1 + side * (tiles - 2)) % tiles),
        )

    blocks = 4

    def last_halo(m, q):
        rows = pl.ds(q * B, B)
        return remote(
            x_ref.at[H - 2 + m, rows], raw.at[X + 2 * H - 2 + m, rows],
            halo_send.at[0], halo_recv.at[2 * H - 2 + blocks * m + q], to(g, left),
        )

    part_at = B

    def third_halo(q):
        rows = pl.ds(q * part_at, part_at - q * (2 * part_at - blocks * B))
        return remote(
            x_ref.at[X - 3, rows], raw.at[H - 3, rows],
            halo_send.at[0], halo_recv.at[2 + q * (2 * H + 4)], to(g, right),
        )

    def start_left():
        for k in range(2):
            halo(0, k).start()
        for q in range(2):
            third_halo(q).start()
        for k in range(3, H):
            halo(0, k).start()

    def start_right():
        for k in range(H - 2):
            halo(1, k).start()
        for m in range(2):
            for q in range(blocks):
                last_halo(m, q).start()

    sub = lax.broadcasted_iota(jnp.int32, (2, 8, 128), 1)
    low = sub < 4
    first = sub % 4 == 0
    last = sub % 4 == 3
    fine = blocks * blocks

    def split(v, p_ref, m_ref, layer, rows):
        square = v * v
        p_ref[layer, rows] = v - square
        m_ref[layer, rows] = v + square

    def convert(layer):
        for i in range(blocks):
            rows = pl.ds(i * B, B)
            split(KAPPA * raw[layer, rows], pa, ma, layer, rows)

    def convert_from(lo, hi):
        def body(i, carry):
            convert(i + H)
            return carry
        lax.fori_loop(lo, hi, body, 0)

    load(0).wait()
    convert_from(0, piece)
    pl.semaphore_wait(barrier, len(others) + jnp.minimum(t, 1))

    @pl.when(t == tiles - 1)
    def _():
        give_credit()

    start_left()

    odd = t % 2

    @pl.when(odd == 1)
    def _():
        start_right()

    for lo in range(piece, 2 * H + 1, piece):
        load(lo // piece).wait()
        convert_from(lo, min(lo + piece, 2 * H + 1))
    load_levels.wait()
    load_sign.wait()

    rates = [ALPHA * rate_of(levels_ref[0, d]) for d in range(6)]
    total = rates[0] + rates[1] + rates[2] + rates[3] + rates[4] + rates[5]
    centre = 0.5 - total
    sign = (2 * sign_ref[0] - 1).astype(jnp.float32) * (1.0 / KAPPA)

    def swapped(v):
        return jnp.concatenate([v[1:2], v[0:1]], 0)

    def at_rows(i):
        return pl.ds(i * 2, 2)

    def stencil(p_ref, m_ref, layer, i, upper):
        rows = at_rows(i)
        p = p_ref[layer, rows]
        m = m_ref[layer, rows]
        p5 = pltpu.roll(p, 127, 2)
        m5 = pltpu.roll(m, 1, 2)
        acc = centre * (p + m)
        if upper:
            acc += rates[0] * (p_ref[layer + 1, rows] + m_ref[layer - 1, rows])
        else:
            acc += rates[0] * m_ref[layer - 1, rows]
        i1, i2 = i // blocks * blocks, i % blocks
        acc += rates[1] * (
            p_ref[layer, at_rows((i + blocks) % fine)]
            + m_ref[layer, at_rows((i + fine - blocks) % fine)]
        )
        acc += rates[2] * (
            p_ref[layer, at_rows(i1 + (i2 + 1) % blocks)]
            + m_ref[layer, at_rows(i1 + (i2 + blocks - 1) % blocks)]
        )
        ph = pltpu.roll(p, 4, 1)
        mh = pltpu.roll(m, 4, 1)
        acc += rates[3] * (jnp.where(low, ph, swapped(ph)) + jnp.where(low, swapped(mh), mh))
        p4 = pltpu.roll(jnp.where(first, ph, p), 7, 1)
        m4 = pltpu.roll(jnp.where(last, mh, m), 1, 1)
        acc += rates[4] * (p4 + m4)
        acc += rates[5] * (p5 + m5)
        return acc, rows

    state = [(pa, ma), (pb, mb)]

    def step(at, layer):
        src, dst = state[at % 2], state[(at + 1) % 2]
        for n in range(fine):
            acc, rows = stencil(*src, layer, n, True)
            if at == STEPS - 1:
                val[layer - H, rows] = sign * acc
            else:
                split(acc, *dst, layer, rows)

    def partly(at, layer):
        for n in range(fine):
            acc, rows = stencil(*state[at % 2], layer, n, False)
            rest[at, rows] = acc

    half = B * blocks // 2
    mine = pl.ds(pl.multiple_of(core * half, half), half)
    theirs = pl.ds(pl.multiple_of((1 - core) * half, half), half)

    inner = X - 2 * H

    def place(n):
        past = jnp.minimum(n // inner, 1)
        done = jnp.minimum(n // (X - H), 1)
        return n + (1 - past) * H + (past - done) * (X - H - 1 - 2 * n)

    def pair_copy(n):
        i = place(n)
        return remote(
            val.at[i, theirs], from_pair.at[i], pair_send.at[0], pair_recv.at[n % 4], to(pair, t)
        )

    def far_copy(n, k):
        i = place(n)
        return remote(
            part.at[i], from_far.at[k - 1, i],
            far_send.at[k - 1], far_recv.at[k - 1, jnp.minimum(n, X - H)], to((g + 2 * k) % grids, t),
        )

    def back_copy(n):
        own = comb.at[place(n), mine]
        group = jnp.minimum(n // (X - H), 1)
        return remote(own, own, back_send.at[0], back_recv.at[group], to(pair, t))

    def backs_done(group, count):
        some = part.at[pl.ds(0, count)]
        remote(some, some, back_send.at[0], back_recv.at[group], to(pair, t)).wait_recv()

    def reduce_pair(n):
        pair_copy(n).wait_recv()
        i = place(n)
        part[i] = val[i, mine] + from_pair[i]
        for k in range(1, far):
            far_copy(n, k).start()

    def reduce_far(n, waited=False):
        if not waited:
            for k in range(1, far):
                far_copy(n, k).wait_recv()
        i = place(n)
        summed = part[i]
        for k in range(1, far):
            summed += from_far[k - 1, i]
        comb[i, mine] = summed
        back_copy(n).start()

    small = B // 2

    def own_rows(q):
        return pl.ds(pl.multiple_of(q * B + core * small, small), small)

    def other_rows(q):
        return pl.ds(pl.multiple_of(q * B + (1 - core) * small, small), small)

    def kept(q):
        return pl.ds(q * small, small)

    def last_pair(m, q):
        i = X - 2 + m
        return remote(
            val.at[i, other_rows(q)], from_pair.at[i, kept(q)],
            pair_send.at[0], pair_recv.at[4 - 4 * m + q], to(pair, t),
        )

    def last_far(m, q, k):
        i = X - 2 + m
        return remote(
            part.at[i, kept(q)], from_far.at[k - 1, i, kept(q)],
            far_send.at[k - 1], far_recv.at[k - 1, X - H + m * (1 + q)], to((g + 2 * k) % grids, t),
        )

    def last_back(m, q):
        own = comb.at[X - 2 + m, own_rows(q)]
        return remote(own, own, back_send.at[0], back_recv.at[1 + m], to(pair, t))

    def reduce_last_pair(m, q):
        i = X - 2 + m
        last_pair(m, q).wait_recv()
        part[i, kept(q)] = val[i, own_rows(q)] + from_pair[i, kept(q)]
        for k in range(1, far):
            last_far(m, q, k).start()

    def reduce_last_far(m, q):
        i = X - 2 + m
        if m == 1:
            for k in range(1, far):
                last_far(m, q, k).wait_recv()
        summed = part[i, kept(q)]
        for k in range(1, far):
            summed += from_far[k - 1, i, kept(q)]
        comb[i, own_rows(q)] = summed
        last_back(m, q).start()

    ahead = [2, 2, 3, 5, 7, 9, 10]
    held = 5

    def done_before(j):
        count = 0
        for i, n in enumerate(ahead):
            more = n - (ahead[i - 1] if i else 0)
            count = count + more * jnp.minimum(jnp.maximum(j - i + 1, 0), 1)
        return jnp.maximum(count, jnp.maximum(1 - t, 0) * held * jnp.minimum(jnp.maximum(j - 1, 0), 1))

    def finish_far(lo, hi):
        def body(n, carry):
            reduce_far(n)
            return carry
        lax.fori_loop(lo, hi, body, 0)

    following = remote(comb.at[0, mine], comb.at[X, mine], back_send.at[0], next_recv.at[0], to(g, left))
    shared = remote(comb.at[X, mine], comb.at[X, mine], back_send.at[0], next_recv.at[1], to(pair, t))

    for s in range(STEPS):
        def body(i, carry, s=s):
            step(s, i + H)
            return carry
        lax.fori_loop(s + 1, 2 * H - s, body, 0)
    pair_copy(0).start()

    def wave(n, carry):
        leftward = n // inner
        back = 1 - 2 * leftward
        at = (1 - leftward) * (n + 2 * H) + leftward * (inner - 1 - n)
        j = n - inner

        @pl.when((leftward == 0) & (at % piece == 0))
        def _():
            load(at // piece).wait()

        @pl.when(leftward == 1)
        def _():
            finish_far(done_before(j - 1), done_before(j))

        @pl.when((t == 0) & (j == 2))
        def _():
            pl.semaphore_wait(credit, 1)
            start_right()

        @pl.when((leftward == 1) & (j != 2))
        def _():
            halo(0, j).wait_recv()

        paced = (odd == 1) & (t < tiles - 1)

        @pl.when((j == 2) & ((odd == 0) | (t == tiles - 1)))
        def _():
            third_halo(0).wait_recv()

        @pl.when(j == 2)
        def _():
            third_halo(1).wait_recv()

        @pl.when(paced & (j == 0))
        def _():
            third_halo(0).wait_recv()
            pl.semaphore_signal(
                met, inc=1, device_id=to(pair, t), device_id_type=pl.DeviceIdType.MESH
            )
            pl.semaphore_wait(met, 1)
            give_credit()

        convert(at + H)
        for s in range(STEPS):
            step(s, at - back * (s + 1) + H)
        pair_copy(n).start()

        @pl.when((odd == 0) & (t > 0) & (j == 1))
        def _():
            pl.semaphore_wait(credit, 1)
            start_right()

        reduce_pair(n - 1)
        return carry

    lax.fori_loop(1, X - H, wave, 0)

    def prepare(n):
        for s in range(STEPS):
            partly(s, n + 2 * H - 1 - s)

    def complete(n, q, keep):
        rows = pl.ds(q * B, B)
        v = KAPPA * raw[n + 2 * H, rows]
        for s in range(STEPS):
            square = v * v
            p = v - square
            if keep:
                p_ref, m_ref = state[s % 2]
                p_ref[n + 2 * H - s, rows] = p
                m_ref[n + 2 * H - s, rows] = v + square
            v = rest[s, rows] + rates[0] * p
        val[n, rows] = sign * v

    def ending(n, carry):
        j = n - inner
        prepare(n)
        reduce_pair(n - 1)
        finish_far(done_before(j - 1), done_before(j))
        halo(1, n - (X - H)).wait_recv()
        for q in range(blocks):
            complete(n, q, True)
        pair_copy(n).start()
        return carry

    lax.fori_loop(X - H, X - 2, ending, 0)
    prepare(X - 2)
    reduce_pair(X - 3)
    finish_far(ahead[-2], ahead[-1])
    for q in range(blocks):
        last_halo(0, q).wait_recv()
        complete(X - 2, q, True)
        last_pair(0, q).start()
        if q > 1:
            reduce_last_pair(0, q - 2)
    finish_far(ahead[-1], X - H)
    following.start()
    reduce_last_pair(0, blocks - 2)
    prepare(X - 1)
    reduce_last_pair(0, blocks - 1)
    for q in range(blocks):
        last_halo(1, q).wait_recv()
        complete(X - 1, q, False)
        last_pair(1, q).start()
    reduce_last_pair(1, 0)

    level = levels_ref[0, 0]
    reach = 8

    def rebuilt(base, rows, top):
        v = {0: comb[base, rows], reach: comb[base + reach, rows]}
        depth, gap = 2, reach // 2
        while gap >= 1:
            for i in range(gap, reach, 2 * gap):
                mean = 0.5 * (v[i - gap] + v[i + gap])
                v[i] = jnp.where(level >= depth, comb[base + i, rows], mean) if i < top else mean
            depth, gap = depth + 1, gap // 2
        return v

    def write(base, top):
        def body(i, carry):
            rows = pl.ds(pl.multiple_of(i * 2, 2), 2)
            v = rebuilt(base, rows, top)
            for j in range(reach):
                o_ref[base + j, rows] = v[j]
            return carry
        lax.fori_loop(0, B * blocks // 2, body, 0, unroll=2)

    backs_done(0, X - H)
    for q in range(X // reach - 1):
        write(q * reach, reach)
    for q in range(1, blocks):
        reduce_last_pair(1, q)
    following.wait_recv()
    shared.start()
    some = part.at[pl.ds(0, H - 1)]
    for k in range(1, far):
        remote(some, some, far_send.at[k - 1], far_recv.at[k - 1, X - H], to(pair, t)).wait_recv()
    for n in range(X - H, X - 2):
        reduce_far(n, True)
    for m in range(2):
        for q in range(blocks):
            reduce_last_far(m, q)
    whole = raw.at[pl.ds(0, 2 * H)]
    remote(whole, whole, halo_send.at[0], halo_recv.at[0], to(g, left)).wait_send()
    backs_done(1, H - 1)
    shared.wait_recv()
    write(X - reach, reach - 1)
    remote(part, part, pair_send.at[0], pair_recv.at[0], to(pair, t)).wait_send()
    backs_done(2, 1)
    for i in range(blocks):
        rows = pl.ds(i * B, B)
        o_ref[X - 1, rows] = jnp.where(level >= 4, comb[X - 1, rows], o_ref[X - 1, rows])
    for k in range(1, far):
        remote(part, part, far_send.at[k - 1], far_recv.at[k - 1, 0], to(pair, t)).wait_send()
    whole = raw.at[pl.ds(0, X // 2 + 1)]
    remote(whole, whole, back_send.at[0], back_recv.at[0], to(pair, t)).wait_send()


def solution(mesh):
    grids, tiles = mesh.shape["grid"], mesh.shape["tile"]

    def on_device(state_field, levels, sign_bits):
        X = state_field.shape[1]
        L = state_field.shape[-1]
        V = state_field.size // (X * 8 * L)
        B = V // state_field.shape[2]
        H = STEPS
        far = grids // 2 - 1
        f32 = jnp.float32
        field = (V, 8, L)
        halved = (V // 2, 8, L)
        dma = pltpu.SemaphoreType.DMA
        state = pltpu.with_memory_space_constraint(state_field.reshape(X, *field), pltpu.HBM)
        levels = pltpu.with_memory_space_constraint(levels, pltpu.HBM)
        result = pl.pallas_call(
            functools.partial(kernel, grids, tiles, X, B),
            out_shape=jax.ShapeDtypeStruct((X, *field), f32),
            in_specs=[pl.BlockSpec(memory_space=pltpu.HBM)] * 3,
            out_specs=pl.BlockSpec(memory_space=pltpu.VMEM),
            scratch_shapes=[
                pltpu.SMEM(levels.shape, jnp.int32),
                pltpu.SMEM(sign_bits.shape, jnp.int32),
                pltpu.VMEM((X + 2 * H, *field), f32),
                pltpu.VMEM((X + 2 * H, *field), f32),
                pltpu.VMEM((X + 2 * H, *field), f32),
                pltpu.VMEM((X + 2 * H, *field), f32),
                pltpu.VMEM((X + 2 * H, *field), f32),
                pltpu.VMEM((H, *field), f32),
                pltpu.VMEM((X, *field), f32),
                pltpu.VMEM((X, *halved), f32),
                pltpu.VMEM((X, *halved), f32),
                pltpu.VMEM((far, X, *halved), f32),
                pltpu.VMEM((X + 1, *field), f32),
                dma((2,)),
                dma((LOADS,)),
                dma((1,)),
                dma((2 * H + 7,)),
                dma((1,)),
                dma((8,)),
                dma((far,)),
                dma((far, X - H + 5)),
                dma((1,)),
                dma((3,)),
                dma((2,)),
                pltpu.SemaphoreType.REGULAR,
                pltpu.SemaphoreType.REGULAR,
            ],
            compiler_params=pltpu.CompilerParams(
                collective_id=0, has_side_effects=True, vmem_limit_bytes=48 * 1024 * 1024
            ),
        )(levels, sign_bits, state)
        return result.reshape(state_field.shape)

    placed = (P("grid", "tile", None, None, None, None, None), P("grid", None), P("grid"))
    return jax.shard_map(
        on_device,
        mesh=mesh,
        in_specs=placed,
        out_specs=P("grid", "tile", None, None, None, None, None),
        check_vma=False,
    )
```

```python
import functools

import jax
import jax.numpy as jnp
from jax import lax
from jax.experimental import pallas as pl
from jax.experimental.pallas import tpu as pltpu
from jax.sharding import PartitionSpec as P

STEPS = 4
ALPHA = 0.08
BETA = 0.0125
KAPPA = BETA / ALPHA
LOADS = 4


def rate_of(level):
    return jnp.where(
        level >= 4, 1.0, jnp.where(level == 3, 0.5, jnp.where(level == 2, 0.25, 0.125))
    ).astype(jnp.float32)


def kernel(
    grids, tiles, X, B,
    levels_hbm, sign_hbm, x_ref, o_ref, stage_ref,
    levels_ref, sign_ref, raw, pa, ma, pb, mb, rest, val, from_pair, part, from_far, comb,
    small_sem, load_sem, halo_send, halo_recv, pair_send, pair_recv, far_send, far_recv,
    back_send, back_recv, next_recv, credit, met,
):
    H = STEPS
    g = lax.axis_index("grid")
    t = lax.axis_index("tile")
    core = g % 2
    pair = g + 1 - 2 * core
    right = (t + 1) % tiles
    left = (t + tiles - 1) % tiles
    far = grids // 2

    def to(grid_at, tile_at):
        return {"grid": grid_at, "tile": tile_at}

    def remote(src, dst, send, recv, where):
        return pltpu.make_async_remote_copy(
            src_ref=src, dst_ref=dst, send_sem=send, recv_sem=recv,
            device_id=where, device_id_type=pl.DeviceIdType.MESH,
        )

    piece = X // LOADS

    def load(i):
        return pltpu.make_async_copy(
            x_ref.at[pl.ds(i * piece, piece)], raw.at[pl.ds(H + i * piece, piece)], load_sem.at[i]
        )

    load_levels = pltpu.make_async_copy(levels_hbm, levels_ref, small_sem.at[0])
    load_sign = pltpu.make_async_copy(sign_hbm, sign_ref, small_sem.at[1])
    load(0).start()
    load_levels.start()
    load_sign.start()
    barrier = pltpu.get_barrier_semaphore()

    def greet(other):
        pl.semaphore_signal(barrier, inc=1, device_id=other, device_id_type=pl.DeviceIdType.MESH)

    others = [to(g, left), to(pair, t)]
    others += [to((g + 2 * k) % grids, t) for k in range(1, far)]
    for other in others:
        greet(other)

    @pl.when(t < tiles - 1)
    def _():
        greet(to(g, right))

    def give_credit():
        pl.semaphore_signal(
            credit, inc=1, device_id=to(g, right), device_id_type=pl.DeviceIdType.MESH
        )

    for i in range(1, LOADS):
        load(i).start()

    def halo(side, k):
        return remote(
            x_ref.at[(1 - side) * (X - 1 - k) + side * k],
            raw.at[(1 - side) * (H - 1 - k) + side * (X + H + k)],
            halo_send.at[0], halo_recv.at[side * H + k],
            to(g, (t + 1 + side * (tiles - 2)) % tiles),
        )

    blocks = 4

    def last_halo(m, q):
        rows = pl.ds(q * B, B)
        return remote(
            x_ref.at[H - 2 + m, rows], raw.at[X + 2 * H - 2 + m, rows],
            halo_send.at[0], halo_recv.at[2 * H - 2 + blocks * m + q], to(g, left),
        )

    part_at = B

    def third_halo(q):
        rows = pl.ds(q * part_at, part_at - q * (2 * part_at - blocks * B))
        return remote(
            x_ref.at[X - 3, rows], raw.at[H - 3, rows],
            halo_send.at[0], halo_recv.at[2 + q * (2 * H + 4)], to(g, right),
        )

    def start_left():
        for k in range(2):
            halo(0, k).start()
        for q in range(2):
            third_halo(q).start()
        for k in range(3, H):
            halo(0, k).start()

    def start_right():
        for k in range(H - 2):
            halo(1, k).start()
        for m in range(2):
            for q in range(blocks):
                last_halo(m, q).start()

    sub = lax.broadcasted_iota(jnp.int32, (2, 8, 128), 1)
    low = sub < 4
    place_in = lax.broadcasted_iota(jnp.int32, (8, 128), 0)
    up = place_in // 4 * 4 + (place_in + 1) % 4
    down = place_in // 4 * 4 + (place_in + 3) % 4

    def turned(v, where):
        return jnp.stack([jnp.take_along_axis(v[i], where, axis=0) for i in range(2)])

    fine = blocks * blocks

    def split(v, p_ref, m_ref, layer, rows):
        square = v * v
        p_ref[layer, rows] = v - square
        m_ref[layer, rows] = v + square

    def convert(layer):
        for i in range(blocks):
            rows = pl.ds(i * B, B)
            split(KAPPA * raw[layer, rows], pa, ma, layer, rows)

    def convert_from(lo, hi):
        def body(i, carry):
            convert(i + H)
            return carry
        lax.fori_loop(lo, hi, body, 0)

    load(0).wait()
    convert_from(0, piece)
    pl.semaphore_wait(barrier, len(others) + jnp.minimum(t, 1))

    @pl.when(t == tiles - 1)
    def _():
        give_credit()

    start_left()

    odd = t % 2

    @pl.when(odd == 1)
    def _():
        start_right()

    for lo in range(piece, 2 * H + 1, piece):
        load(lo // piece).wait()
        convert_from(lo, min(lo + piece, 2 * H + 1))
    load_levels.wait()
    load_sign.wait()

    rates = [ALPHA * rate_of(levels_ref[0, d]) for d in range(6)]
    total = rates[0] + rates[1] + rates[2] + rates[3] + rates[4] + rates[5]
    centre = 0.5 - total
    sign = (2 * sign_ref[0] - 1).astype(jnp.float32) * (1.0 / KAPPA)

    def swapped(v):
        return jnp.concatenate([v[1:2], v[0:1]], 0)

    def at_rows(i):
        return pl.ds(i * 2, 2)

    def stencil(p_ref, m_ref, layer, i, upper):
        rows = at_rows(i)
        p = p_ref[layer, rows]
        m = m_ref[layer, rows]
        p5 = pltpu.roll(p, 127, 2)
        m5 = pltpu.roll(m, 1, 2)
        acc = centre * (p + m)
        if upper:
            acc += rates[0] * (p_ref[layer + 1, rows] + m_ref[layer - 1, rows])
        else:
            acc += rates[0] * m_ref[layer - 1, rows]
        i1, i2 = i // blocks * blocks, i % blocks
        acc += rates[1] * (
            p_ref[layer, at_rows((i + blocks) % fine)]
            + m_ref[layer, at_rows((i + fine - blocks) % fine)]
        )
        acc += rates[2] * (
            p_ref[layer, at_rows(i1 + (i2 + 1) % blocks)]
            + m_ref[layer, at_rows(i1 + (i2 + blocks - 1) % blocks)]
        )
        crossed = jnp.where(low, swapped(p), p) + jnp.where(low, m, swapped(m))
        acc += rates[3] * pltpu.roll(crossed, 4, 1)
        acc += rates[4] * (turned(p, up) + turned(m, down))
        acc += rates[5] * (p5 + m5)
        return acc, rows

    state = [(pa, ma), (pb, mb)]

    def step(at, layer):
        src, dst = state[at % 2], state[(at + 1) % 2]
        for n in range(fine):
            acc, rows = stencil(*src, layer, n, True)
            if at == STEPS - 1:
                val[layer - H, rows] = sign * acc
            else:
                split(acc, *dst, layer, rows)

    def partly(at, layer):
        for n in range(fine):
            acc, rows = stencil(*state[at % 2], layer, n, False)
            rest[at, rows] = acc

    half = B * blocks // 2
    mine = pl.ds(pl.multiple_of(core * half, half), half)
    theirs = pl.ds(pl.multiple_of((1 - core) * half, half), half)

    inner = X - 2 * H

    def place(n):
        past = jnp.minimum(n // inner, 1)
        done = jnp.minimum(n // (X - H), 1)
        return n + (1 - past) * H + (past - done) * (X - H - 1 - 2 * n)

    def pair_copy(n):
        i = place(n)
        return remote(
            val.at[i, theirs], from_pair.at[i], pair_send.at[0], pair_recv.at[n % 4], to(pair, t)
        )

    def far_copy(n, k):
        i = place(n)
        return remote(
            part.at[i], from_far.at[k - 1, i],
            far_send.at[k - 1], far_recv.at[k - 1, jnp.minimum(n, X - H)], to((g + 2 * k) % grids, t),
        )

    def back_copy(n):
        own = comb.at[place(n), mine]
        group = jnp.minimum(n // (X - H), 1)
        return remote(own, own, back_send.at[0], back_recv.at[group], to(pair, t))

    def backs_done(group, count):
        some = part.at[pl.ds(0, count)]
        remote(some, some, back_send.at[0], back_recv.at[group], to(pair, t)).wait_recv()

    def reduce_pair(n):
        pair_copy(n).wait_recv()
        i = place(n)
        part[i] = val[i, mine] + from_pair[i]
        for k in range(1, far):
            far_copy(n, k).start()

    def reduce_far(n, waited=False):
        if not waited:
            for k in range(1, far):
                far_copy(n, k).wait_recv()
        i = place(n)
        summed = part[i]
        for k in range(1, far):
            summed += from_far[k - 1, i]
        comb[i, mine] = summed
        back_copy(n).start()

    small = B // 2

    def own_rows(q):
        return pl.ds(pl.multiple_of(q * B + core * small, small), small)

    def other_rows(q):
        return pl.ds(pl.multiple_of(q * B + (1 - core) * small, small), small)

    def kept(q):
        return pl.ds(q * small, small)

    def last_pair(m, q):
        i = X - 2 + m
        return remote(
            val.at[i, other_rows(q)], from_pair.at[i, kept(q)],
            pair_send.at[0], pair_recv.at[4 - 4 * m + q], to(pair, t),
        )

    def last_far(m, q, k):
        i = X - 2 + m
        return remote(
            part.at[i, kept(q)], from_far.at[k - 1, i, kept(q)],
            far_send.at[k - 1], far_recv.at[k - 1, X - H + m * (1 + q)], to((g + 2 * k) % grids, t),
        )

    def last_back(m, q):
        own = comb.at[X - 2 + m, own_rows(q)]
        return remote(own, own, back_send.at[0], back_recv.at[1 + m], to(pair, t))

    def reduce_last_pair(m, q):
        i = X - 2 + m
        last_pair(m, q).wait_recv()
        part[i, kept(q)] = val[i, own_rows(q)] + from_pair[i, kept(q)]
        for k in range(1, far):
            last_far(m, q, k).start()

    def reduce_last_far(m, q):
        i = X - 2 + m
        if m == 1:
            for k in range(1, far):
                last_far(m, q, k).wait_recv()
        summed = part[i, kept(q)]
        for k in range(1, far):
            summed += from_far[k - 1, i, kept(q)]
        comb[i, own_rows(q)] = summed
        last_back(m, q).start()

    ahead = [2, 2, 3, 5, 7, 9, 10]
    held = 5

    def done_before(j):
        count = 0
        for i, n in enumerate(ahead):
            more = n - (ahead[i - 1] if i else 0)
            count = count + more * jnp.minimum(jnp.maximum(j - i + 1, 0), 1)
        return jnp.maximum(count, jnp.maximum(1 - t, 0) * held * jnp.minimum(jnp.maximum(j - 1, 0), 1))

    def finish_far(lo, hi):
        def body(n, carry):
            reduce_far(n)
            return carry
        lax.fori_loop(lo, hi, body, 0)

    staged = pltpu.make_async_copy(comb.at[0, mine], stage_ref, small_sem.at[0])
    following = remote(stage_ref, comb.at[X, mine], back_send.at[0], next_recv.at[0], to(g, left))
    shared = remote(comb.at[X, mine], comb.at[X, mine], back_send.at[0], next_recv.at[1], to(pair, t))

    for s in range(STEPS):
        def body(i, carry, s=s):
            step(s, i + H)
            return carry
        lax.fori_loop(s + 1, 2 * H - s, body, 0)
    pair_copy(0).start()

    def wave(n, carry):
        leftward = n // inner
        back = 1 - 2 * leftward
        at = (1 - leftward) * (n + 2 * H) + leftward * (inner - 1 - n)
        j = n - inner

        @pl.when((leftward == 0) & (at % piece == 0))
        def _():
            load(at // piece).wait()

        @pl.when(leftward == 1)
        def _():
            finish_far(done_before(j - 1), done_before(j))

        @pl.when((t == 0) & (j == 2))
        def _():
            pl.semaphore_wait(credit, 1)
            start_right()

        @pl.when((leftward == 1) & (j != 2))
        def _():
            halo(0, j).wait_recv()

        paced = (odd == 1) & (t < tiles - 1)

        @pl.when((j == 2) & ((odd == 0) | (t == tiles - 1)))
        def _():
            third_halo(0).wait_recv()

        @pl.when(j == 2)
        def _():
            third_halo(1).wait_recv()

        @pl.when(paced & (j == 0))
        def _():
            third_halo(0).wait_recv()
            pl.semaphore_signal(
                met, inc=1, device_id=to(pair, t), device_id_type=pl.DeviceIdType.MESH
            )
            pl.semaphore_wait(met, 1)
            give_credit()

        convert(at + H)
        for s in range(STEPS):
            step(s, at - back * (s + 1) + H)
            if s == 1:
                @pl.when((n == 1) & (core == 0))
                def _():
                    reduce_pair(0)
        pair_copy(n).start()

        @pl.when((odd == 0) & (t > 0) & (j == 1))
        def _():
            pl.semaphore_wait(credit, 1)
            start_right()

        @pl.when((n > 1) | (core == 1))
        def _():
            reduce_pair(n - 1)
        return carry

    lax.fori_loop(1, X - H, wave, 0)

    def prepare(n):
        for s in range(STEPS):
            partly(s, n + 2 * H - 1 - s)

    def complete(n, q, keep):
        rows = pl.ds(q * B, B)
        v = KAPPA * raw[n + 2 * H, rows]
        for s in range(STEPS):
            square = v * v
            p = v - square
            if keep:
                p_ref, m_ref = state[s % 2]
                p_ref[n + 2 * H - s, rows] = p
                m_ref[n + 2 * H - s, rows] = v + square
            v = rest[s, rows] + rates[0] * p
        val[n, rows] = sign * v

    def ending(n, carry):
        j = n - inner
        prepare(n)
        reduce_pair(n - 1)
        finish_far(done_before(j - 1), done_before(j))
        halo(1, n - (X - H)).wait_recv()
        for q in range(blocks):
            complete(n, q, True)
        pair_copy(n).start()
        return carry

    lax.fori_loop(X - H, X - 2, ending, 0)
    prepare(X - 2)
    reduce_pair(X - 3)
    finish_far(ahead[-2], ahead[-1])
    for q in range(blocks):
        last_halo(0, q).wait_recv()
        complete(X - 2, q, True)
        last_pair(0, q).start()
        if q > 1:
            reduce_last_pair(0, q - 2)
    finish_far(ahead[-1], X - H)
    staged.start()
    reduce_last_pair(0, blocks - 2)
    prepare(X - 1)
    staged.wait()
    following.start()
    reduce_last_pair(0, blocks - 1)
    for q in range(blocks):
        last_halo(1, q).wait_recv()
        complete(X - 1, q, False)
        last_pair(1, q).start()
    reduce_last_pair(1, 0)

    level = levels_ref[0, 0]
    reach = 8

    def rebuilt(base, rows, top):
        v = {0: comb[base, rows], reach: comb[base + reach, rows]}
        depth, gap = 2, reach // 2
        while gap >= 1:
            for i in range(gap, reach, 2 * gap):
                mean = 0.5 * (v[i - gap] + v[i + gap])
                v[i] = jnp.where(level >= depth, comb[base + i, rows], mean) if i < top else mean
            depth, gap = depth + 1, gap // 2
        return v

    def write(base, top):
        def body(i, carry):
            rows = pl.ds(pl.multiple_of(i * 2, 2), 2)
            v = rebuilt(base, rows, top)
            for j in range(reach):
                o_ref[base + j, rows] = v[j]
            return carry
        lax.fori_loop(0, B * blocks // 2, body, 0, unroll=2)

    backs_done(0, X - H)
    for q in range(X // reach - 1):
        write(q * reach, reach)
    for q in range(1, blocks):
        reduce_last_pair(1, q)
    following.wait_recv()
    shared.start()
    some = part.at[pl.ds(0, H - 1)]
    for k in range(1, far):
        remote(some, some, far_send.at[k - 1], far_recv.at[k - 1, X - H], to(pair, t)).wait_recv()
    for n in range(X - H, X - 2):
        reduce_far(n, True)
    for m in range(2):
        for q in range(blocks):
            reduce_last_far(m, q)
    whole = raw.at[pl.ds(0, 2 * H)]
    remote(whole, whole, halo_send.at[0], halo_recv.at[0], to(g, left)).wait_send()
    backs_done(1, H - 1)
    shared.wait_recv()
    write(X - reach, reach - 1)
    remote(part, part, pair_send.at[0], pair_recv.at[0], to(pair, t)).wait_send()
    backs_done(2, 1)
    for i in range(blocks):
        rows = pl.ds(i * B, B)
        o_ref[X - 1, rows] = jnp.where(level >= 4, comb[X - 1, rows], o_ref[X - 1, rows])
    for k in range(1, far):
        remote(part, part, far_send.at[k - 1], far_recv.at[k - 1, 0], to(pair, t)).wait_send()
    whole = raw.at[pl.ds(0, X // 2 + 1)]
    remote(whole, whole, back_send.at[0], back_recv.at[0], to(pair, t)).wait_send()


def solution(mesh):
    grids, tiles = mesh.shape["grid"], mesh.shape["tile"]

    def on_device(state_field, levels, sign_bits):
        X = state_field.shape[1]
        L = state_field.shape[-1]
        V = state_field.size // (X * 8 * L)
        B = V // state_field.shape[2]
        H = STEPS
        far = grids // 2 - 1
        f32 = jnp.float32
        field = (V, 8, L)
        halved = (V // 2, 8, L)
        dma = pltpu.SemaphoreType.DMA
        state = pltpu.with_memory_space_constraint(state_field.reshape(X, *field), pltpu.HBM)
        levels = pltpu.with_memory_space_constraint(levels, pltpu.HBM)
        result, _ = pl.pallas_call(
            functools.partial(kernel, grids, tiles, X, B),
            out_shape=[jax.ShapeDtypeStruct((X, *field), f32), pltpu.HBM(halved, f32)],
            in_specs=[pl.BlockSpec(memory_space=pltpu.HBM)] * 3,
            out_specs=[pl.BlockSpec(memory_space=pltpu.VMEM), pl.BlockSpec(memory_space=pltpu.HBM)],
            scratch_shapes=[
                pltpu.SMEM(levels.shape, jnp.int32),
                pltpu.SMEM(sign_bits.shape, jnp.int32),
                pltpu.VMEM((X + 2 * H, *field), f32),
                pltpu.VMEM((X + 2 * H, *field), f32),
                pltpu.VMEM((X + 2 * H, *field), f32),
                pltpu.VMEM((X + 2 * H, *field), f32),
                pltpu.VMEM((X + 2 * H, *field), f32),
                pltpu.VMEM((H, *field), f32),
                pltpu.VMEM((X, *field), f32),
                pltpu.VMEM((X, *halved), f32),
                pltpu.VMEM((X, *halved), f32),
                pltpu.VMEM((far, X, *halved), f32),
                pltpu.VMEM((X + 1, *field), f32),
                dma((2,)),
                dma((LOADS,)),
                dma((1,)),
                dma((2 * H + 7,)),
                dma((1,)),
                dma((8,)),
                dma((far,)),
                dma((far, X - H + 5)),
                dma((1,)),
                dma((3,)),
                dma((2,)),
                pltpu.SemaphoreType.REGULAR,
                pltpu.SemaphoreType.REGULAR,
            ],
            compiler_params=pltpu.CompilerParams(
                collective_id=0, has_side_effects=True, vmem_limit_bytes=48 * 1024 * 1024
            ),
        )(levels, sign_bits, state)
        return result.reshape(state_field.shape)

    placed = (P("grid", "tile", None, None, None, None, None), P("grid", None), P("grid"))
    return jax.shard_map(
        on_device,
        mesh=mesh,
        in_specs=placed,
        out_specs=P("grid", "tile", None, None, None, None, None),
        check_vma=False,
    )
```

```python
import functools

import jax
import jax.numpy as jnp
from jax import lax
from jax.experimental import pallas as pl
from jax.experimental.pallas import tpu as pltpu
from jax.sharding import PartitionSpec as P

STEPS = 4
ALPHA = 0.08
BETA = 0.0125
KAPPA = BETA / ALPHA
LOADS = 4


def rate_of(level):
    return jnp.where(
        level >= 4, 1.0, jnp.where(level == 3, 0.5, jnp.where(level == 2, 0.25, 0.125))
    ).astype(jnp.float32)


def kernel(
    grids, tiles, X, B,
    levels_hbm, sign_ref, x_ref, o_ref, stage_ref,
    levels_ref, raw, pa, ma, pb, mb, rest, val, from_pair, part, from_far, comb,
    small_sem, load_sem, halo_send, halo_recv, pair_send, pair_recv, far_send, far_recv,
    back_send, back_recv, next_recv, credit, met,
):
    H = STEPS
    g = lax.axis_index("grid")
    t = lax.axis_index("tile")
    core = g % 2
    pair = g + 1 - 2 * core
    right = (t + 1) % tiles
    left = (t + tiles - 1) % tiles
    far = grids // 2

    def to(grid_at, tile_at):
        return {"grid": grid_at, "tile": tile_at}

    def remote(src, dst, send, recv, where):
        return pltpu.make_async_remote_copy(
            src_ref=src, dst_ref=dst, send_sem=send, recv_sem=recv,
            device_id=where, device_id_type=pl.DeviceIdType.MESH,
        )

    piece = X // LOADS

    def load(i):
        return pltpu.make_async_copy(
            x_ref.at[pl.ds(i * piece, piece)], raw.at[pl.ds(H + i * piece, piece)], load_sem.at[i]
        )

    load_levels = pltpu.make_async_copy(levels_hbm, levels_ref, small_sem.at[0])
    load(0).start()
    load_levels.start()
    barrier = pltpu.get_barrier_semaphore()

    def greet(other):
        pl.semaphore_signal(barrier, inc=1, device_id=other, device_id_type=pl.DeviceIdType.MESH)

    others = [to(g, left), to(pair, t)]
    others += [to((g + 2 * k) % grids, t) for k in range(1, far)]
    for other in others:
        greet(other)

    @pl.when(t < tiles - 1)
    def _():
        greet(to(g, right))

    def give_credit():
        pl.semaphore_signal(
            credit, inc=1, device_id=to(g, right), device_id_type=pl.DeviceIdType.MESH
        )

    for i in range(1, LOADS):
        load(i).start()

    def halo(side, k):
        return remote(
            x_ref.at[(1 - side) * (X - 1 - k) + side * k],
            raw.at[(1 - side) * (H - 1 - k) + side * (X + H + k)],
            halo_send.at[0], halo_recv.at[side * H + k],
            to(g, (t + 1 + side * (tiles - 2)) % tiles),
        )

    blocks = 4

    def last_halo(m, q):
        rows = pl.ds(q * B, B)
        return remote(
            x_ref.at[H - 2 + m, rows], raw.at[X + 2 * H - 2 + m, rows],
            halo_send.at[0], halo_recv.at[2 * H - 2 + blocks * m + q], to(g, left),
        )

    part_at = B

    def third_halo(q):
        rows = pl.ds(q * part_at, part_at - q * (2 * part_at - blocks * B))
        return remote(
            x_ref.at[X - 3, rows], raw.at[H - 3, rows],
            halo_send.at[0], halo_recv.at[2 + q * (2 * H + 4)], to(g, right),
        )

    def start_left():
        for k in range(2):
            halo(0, k).start()
        for q in range(2):
            third_halo(q).start()
        for k in range(3, H):
            halo(0, k).start()

    def start_right():
        for k in range(H - 2):
            halo(1, k).start()
        for m in range(2):
            for q in range(blocks):
                last_halo(m, q).start()

    sub = lax.broadcasted_iota(jnp.int32, (2, 8, 128), 1)
    low = sub < 4
    place_in = lax.broadcasted_iota(jnp.int32, (8, 128), 0)
    up = place_in // 4 * 4 + (place_in + 1) % 4
    down = place_in // 4 * 4 + (place_in + 3) % 4

    def turned(v, where):
        return jnp.stack([jnp.take_along_axis(v[i], where, axis=0) for i in range(2)])

    fine = blocks * blocks

    def split(v, p_ref, m_ref, layer, rows):
        square = v * v
        p_ref[layer, rows] = v - square
        m_ref[layer, rows] = v + square

    def convert(layer):
        for i in range(blocks):
            rows = pl.ds(i * B, B)
            split(KAPPA * raw[layer, rows], pa, ma, layer, rows)

    def convert_from(lo, hi):
        def body(i, carry):
            convert(i + H)
            return carry
        lax.fori_loop(lo, hi, body, 0)

    load(0).wait()
    convert_from(0, piece)
    pl.semaphore_wait(barrier, len(others) + jnp.minimum(t, 1))

    @pl.when(t == tiles - 1)
    def _():
        give_credit()

    start_left()

    odd = t % 2

    @pl.when(odd == 1)
    def _():
        start_right()

    for lo in range(piece, 2 * H + 1, piece):
        load(lo // piece).wait()
        convert_from(lo, min(lo + piece, 2 * H + 1))
    load_levels.wait()

    rates = [ALPHA * rate_of(levels_ref[0, d]) for d in range(6)]
    total = rates[0] + rates[1] + rates[2] + rates[3] + rates[4] + rates[5]
    centre = 0.5 - total
    sign = (2 * sign_ref[0] - 1).astype(jnp.float32) * (1.0 / KAPPA)

    def swapped(v):
        return jnp.concatenate([v[1:2], v[0:1]], 0)

    def at_rows(i):
        return pl.ds(i * 2, 2)

    def stencil(p_ref, m_ref, layer, i, upper):
        rows = at_rows(i)
        p = p_ref[layer, rows]
        m = m_ref[layer, rows]
        p5 = pltpu.roll(p, 127, 2)
        m5 = pltpu.roll(m, 1, 2)
        acc = centre * (p + m)
        if upper:
            acc += rates[0] * (p_ref[layer + 1, rows] + m_ref[layer - 1, rows])
        else:
            acc += rates[0] * m_ref[layer - 1, rows]
        i1, i2 = i // blocks * blocks, i % blocks
        acc += rates[1] * (
            p_ref[layer, at_rows((i + blocks) % fine)]
            + m_ref[layer, at_rows((i + fine - blocks) % fine)]
        )
        acc += rates[2] * (
            p_ref[layer, at_rows(i1 + (i2 + 1) % blocks)]
            + m_ref[layer, at_rows(i1 + (i2 + blocks - 1) % blocks)]
        )
        crossed = jnp.where(low, swapped(p), p) + jnp.where(low, m, swapped(m))
        acc += rates[3] * pltpu.roll(crossed, 4, 1)
        acc += rates[4] * (turned(p, up) + turned(m, down))
        acc += rates[5] * (p5 + m5)
        return acc, rows

    state = [(pa, ma), (pb, mb)]

    def step(at, layer):
        src, dst = state[at % 2], state[(at + 1) % 2]
        for n in range(fine):
            acc, rows = stencil(*src, layer, n, True)
            if at == STEPS - 1:
                val[layer - H, rows] = sign * acc
            else:
                split(acc, *dst, layer, rows)

    def partly(at, layer):
        for n in range(fine):
            acc, rows = stencil(*state[at % 2], layer, n, False)
            rest[at, rows] = acc

    half = B * blocks // 2
    mine = pl.ds(pl.multiple_of(core * half, half), half)
    theirs = pl.ds(pl.multiple_of((1 - core) * half, half), half)

    inner = X - 2 * H

    def place(n):
        past = jnp.minimum(n // inner, 1)
        done = jnp.minimum(n // (X - H), 1)
        return n + (1 - past) * H + (past - done) * (X - H - 1 - 2 * n)

    def pair_copy(n):
        i = place(n)
        return remote(
            val.at[i, theirs], from_pair.at[i], pair_send.at[0], pair_recv.at[n % 4], to(pair, t)
        )

    def far_copy(n, k):
        i = place(n)
        return remote(
            part.at[i], from_far.at[k - 1, i],
            far_send.at[k - 1], far_recv.at[k - 1, jnp.minimum(n, X - H)], to((g + 2 * k) % grids, t),
        )

    def back_copy(n):
        own = comb.at[place(n), mine]
        group = jnp.minimum(n // (X - H), 1)
        return remote(own, own, back_send.at[0], back_recv.at[group], to(pair, t))

    def backs_done(group, count):
        some = part.at[pl.ds(0, count)]
        remote(some, some, back_send.at[0], back_recv.at[group], to(pair, t)).wait_recv()

    def reduce_pair(n):
        pair_copy(n).wait_recv()
        i = place(n)
        part[i] = val[i, mine] + from_pair[i]
        for k in range(1, far):
            far_copy(n, k).start()

    def reduce_far(n, waited=False):
        if not waited:
            for k in range(1, far):
                far_copy(n, k).wait_recv()
        i = place(n)
        summed = part[i]
        for k in range(1, far):
            summed += from_far[k - 1, i]
        comb[i, mine] = summed
        back_copy(n).start()

    small = B // 2

    def own_rows(q):
        return pl.ds(pl.multiple_of(q * B + core * small, small), small)

    def other_rows(q):
        return pl.ds(pl.multiple_of(q * B + (1 - core) * small, small), small)

    def kept(q):
        return pl.ds(q * small, small)

    def last_pair(m, q):
        i = X - 2 + m
        return remote(
            val.at[i, other_rows(q)], from_pair.at[i, kept(q)],
            pair_send.at[0], pair_recv.at[4 - 4 * m + q], to(pair, t),
        )

    def last_far(m, q, k):
        i = X - 2 + m
        return remote(
            part.at[i, kept(q)], from_far.at[k - 1, i, kept(q)],
            far_send.at[k - 1], far_recv.at[k - 1, X - H + m * (1 + q)], to((g + 2 * k) % grids, t),
        )

    def last_back(m, q):
        own = comb.at[X - 2 + m, own_rows(q)]
        return remote(own, own, back_send.at[0], back_recv.at[1 + m], to(pair, t))

    def reduce_last_pair(m, q):
        i = X - 2 + m
        last_pair(m, q).wait_recv()
        part[i, kept(q)] = val[i, own_rows(q)] + from_pair[i, kept(q)]
        for k in range(1, far):
            last_far(m, q, k).start()

    def reduce_last_far(m, q):
        i = X - 2 + m
        if m == 1:
            for k in range(1, far):
                last_far(m, q, k).wait_recv()
        summed = part[i, kept(q)]
        for k in range(1, far):
            summed += from_far[k - 1, i, kept(q)]
        comb[i, own_rows(q)] = summed
        last_back(m, q).start()

    ahead = [2, 2, 3, 5, 7, 9, 10]
    held = 5

    def done_before(j):
        count = 0
        for i, n in enumerate(ahead):
            more = n - (ahead[i - 1] if i else 0)
            count = count + more * jnp.minimum(jnp.maximum(j - i + 1, 0), 1)
        return jnp.maximum(count, jnp.maximum(1 - t, 0) * held * jnp.minimum(jnp.maximum(j - 1, 0), 1))

    def finish_far(lo, hi):
        def body(n, carry):
            reduce_far(n)
            return carry
        lax.fori_loop(lo, hi, body, 0)

    staged = pltpu.make_async_copy(comb.at[0, mine], stage_ref, small_sem.at[0])
    following = remote(stage_ref, comb.at[X, mine], back_send.at[0], next_recv.at[0], to(g, left))
    shared = remote(comb.at[X, mine], comb.at[X, mine], back_send.at[0], next_recv.at[1], to(pair, t))

    for s in range(STEPS):
        def body(i, carry, s=s):
            step(s, i + H)
            return carry
        lax.fori_loop(s + 1, 2 * H - s, body, 0)
    pair_copy(0).start()

    def wave(n, carry):
        leftward = n // inner
        back = 1 - 2 * leftward
        at = (1 - leftward) * (n + 2 * H) + leftward * (inner - 1 - n)
        j = n - inner

        @pl.when((leftward == 0) & (at % piece == 0))
        def _():
            load(at // piece).wait()

        @pl.when(leftward == 1)
        def _():
            finish_far(done_before(j - 1), done_before(j))

        @pl.when((t == 0) & (j == 2))
        def _():
            pl.semaphore_wait(credit, 1)
            start_right()

        @pl.when((leftward == 1) & (j != 2))
        def _():
            halo(0, j).wait_recv()

        paced = (odd == 1) & (t < tiles - 1)

        @pl.when((j == 2) & ((odd == 0) | (t == tiles - 1)))
        def _():
            third_halo(0).wait_recv()

        @pl.when(j == 2)
        def _():
            third_halo(1).wait_recv()

        @pl.when(paced & (j == 0))
        def _():
            third_halo(0).wait_recv()
            pl.semaphore_signal(
                met, inc=1, device_id=to(pair, t), device_id_type=pl.DeviceIdType.MESH
            )
            pl.semaphore_wait(met, 1)
            give_credit()

        convert(at + H)
        for s in range(STEPS):
            step(s, at - back * (s + 1) + H)
            if s == 1:
                @pl.when((n == 1) & (core == 0))
                def _():
                    reduce_pair(0)
        pair_copy(n).start()

        @pl.when((odd == 0) & (t > 0) & (j == 1))
        def _():
            pl.semaphore_wait(credit, 1)
            start_right()

        @pl.when((n > 1) | (core == 1))
        def _():
            reduce_pair(n - 1)
        return carry

    lax.fori_loop(1, X - H, wave, 0)

    def prepare(n):
        for s in range(STEPS):
            partly(s, n + 2 * H - 1 - s)

    def complete(n, q, keep):
        rows = pl.ds(q * B, B)
        v = KAPPA * raw[n + 2 * H, rows]
        for s in range(STEPS):
            square = v * v
            p = v - square
            if keep:
                p_ref, m_ref = state[s % 2]
                p_ref[n + 2 * H - s, rows] = p
                m_ref[n + 2 * H - s, rows] = v + square
            v = rest[s, rows] + rates[0] * p
        val[n, rows] = sign * v

    def ending(n, carry):
        j = n - inner
        prepare(n)
        reduce_pair(n - 1)
        finish_far(done_before(j - 1), done_before(j))
        halo(1, n - (X - H)).wait_recv()
        for q in range(blocks):
            complete(n, q, True)
        pair_copy(n).start()
        return carry

    lax.fori_loop(X - H, X - 2, ending, 0)
    prepare(X - 2)
    reduce_pair(X - 3)
    finish_far(ahead[-2], ahead[-1])
    for q in range(blocks):
        last_halo(0, q).wait_recv()
        complete(X - 2, q, True)
        last_pair(0, q).start()
        if q > 1:
            reduce_last_pair(0, q - 2)
    finish_far(ahead[-1], X - H)
    staged.start()
    reduce_last_pair(0, blocks - 2)
    prepare(X - 1)
    staged.wait()
    following.start()
    reduce_last_pair(0, blocks - 1)
    for q in range(blocks):
        last_halo(1, q).wait_recv()
        complete(X - 1, q, False)
        last_pair(1, q).start()
    reduce_last_pair(1, 0)

    level = levels_ref[0, 0]
    reach = 8

    def rebuilt(base, rows, top):
        v = {0: comb[base, rows], reach: comb[base + reach, rows]}
        depth, gap = 2, reach // 2
        while gap >= 1:
            for i in range(gap, reach, 2 * gap):
                mean = 0.5 * (v[i - gap] + v[i + gap])
                v[i] = jnp.where(level >= depth, comb[base + i, rows], mean) if i < top else mean
            depth, gap = depth + 1, gap // 2
        return v

    def write(base, top):
        def body(i, carry):
            rows = pl.ds(pl.multiple_of(i * 2, 2), 2)
            v = rebuilt(base, rows, top)
            for j in range(reach):
                o_ref[base + j, rows] = v[j]
            return carry
        lax.fori_loop(0, B * blocks // 2, body, 0, unroll=2)

    backs_done(0, X - H)
    for q in range(X // reach - 1):
        write(q * reach, reach)
    for q in range(1, blocks):
        reduce_last_pair(1, q)
    following.wait_recv()
    shared.start()
    some = part.at[pl.ds(0, H - 1)]
    for k in range(1, far):
        remote(some, some, far_send.at[k - 1], far_recv.at[k - 1, X - H], to(pair, t)).wait_recv()
    for n in range(X - H, X - 2):
        reduce_far(n, True)
    for m in range(2):
        for q in range(blocks):
            reduce_last_far(m, q)
    whole = raw.at[pl.ds(0, 2 * H)]
    remote(whole, whole, halo_send.at[0], halo_recv.at[0], to(g, left)).wait_send()
    backs_done(1, H - 1)
    shared.wait_recv()
    write(X - reach, reach - 1)
    remote(part, part, pair_send.at[0], pair_recv.at[0], to(pair, t)).wait_send()
    backs_done(2, 1)
    for i in range(blocks):
        rows = pl.ds(i * B, B)
        o_ref[X - 1, rows] = jnp.where(level >= 4, comb[X - 1, rows], o_ref[X - 1, rows])
    for k in range(1, far):
        remote(part, part, far_send.at[k - 1], far_recv.at[k - 1, 0], to(pair, t)).wait_send()
    whole = raw.at[pl.ds(0, X // 2 + 1)]
    remote(whole, whole, back_send.at[0], back_recv.at[0], to(pair, t)).wait_send()


def solution(mesh):
    grids, tiles = mesh.shape["grid"], mesh.shape["tile"]

    def on_device(state_field, levels, sign_bits):
        X = state_field.shape[1]
        L = state_field.shape[-1]
        V = state_field.size // (X * 8 * L)
        B = V // state_field.shape[2]
        H = STEPS
        far = grids // 2 - 1
        f32 = jnp.float32
        field = (V, 8, L)
        halved = (V // 2, 8, L)
        dma = pltpu.SemaphoreType.DMA
        state = pltpu.with_memory_space_constraint(state_field.reshape(X, *field), pltpu.HBM)
        levels = pltpu.with_memory_space_constraint(levels, pltpu.HBM)
        result, _ = pl.pallas_call(
            functools.partial(kernel, grids, tiles, X, B),
            out_shape=[jax.ShapeDtypeStruct((X, *field), f32), pltpu.HBM(halved, f32)],
            in_specs=[pl.BlockSpec(memory_space=m) for m in (pltpu.HBM, pltpu.SMEM, pltpu.HBM)],
            out_specs=[pl.BlockSpec(memory_space=pltpu.VMEM), pl.BlockSpec(memory_space=pltpu.HBM)],
            scratch_shapes=[
                pltpu.SMEM(levels.shape, jnp.int32),
                pltpu.VMEM((X + 2 * H, *field), f32),
                pltpu.VMEM((X + 2 * H, *field), f32),
                pltpu.VMEM((X + 2 * H, *field), f32),
                pltpu.VMEM((X + 2 * H, *field), f32),
                pltpu.VMEM((X + 2 * H, *field), f32),
                pltpu.VMEM((H, *field), f32),
                pltpu.VMEM((X, *field), f32),
                pltpu.VMEM((X, *halved), f32),
                pltpu.VMEM((X, *halved), f32),
                pltpu.VMEM((far, X, *halved), f32),
                pltpu.VMEM((X + 1, *field), f32),
                dma((1,)),
                dma((LOADS,)),
                dma((1,)),
                dma((2 * H + 7,)),
                dma((1,)),
                dma((8,)),
                dma((far,)),
                dma((far, X - H + 5)),
                dma((1,)),
                dma((3,)),
                dma((2,)),
                pltpu.SemaphoreType.REGULAR,
                pltpu.SemaphoreType.REGULAR,
            ],
            compiler_params=pltpu.CompilerParams(
                collective_id=0, has_side_effects=True, vmem_limit_bytes=48 * 1024 * 1024
            ),
        )(levels, sign_bits, state)
        return result.reshape(state_field.shape)

    placed = (P("grid", "tile", None, None, None, None, None), P("grid", None), P("grid"))
    return jax.shard_map(
        on_device,
        mesh=mesh,
        in_specs=placed,
        out_specs=P("grid", "tile", None, None, None, None, None),
        check_vma=False,
    )
```
